512 devices in a mesh: box: 512 (over z, y, x, core).
Axes of the slice: x: 4, y: 4, z: 16, core: 2. Of those that a mesh axis runs over, the one named last changes fastest.
Arguments:
- cell_state: float32 [1024, 5, 32, 1024], P('box'), as said below
- swap_slots: int32 [512], P('box'), may hold values from 0 to 1, as said below
- neighbours: int32 [1024, 3], P('box'), may hold values from -1 to 1023, as said below
Outputs:
- new_state: float32 [1024, 5, 32, 1024], P('box')
The draws below stay inside these ranges and needn't reach their ends.
Inputs may be any that keep to these rules, and one draw needn't show every extreme that they name: `swap_slots`: each device names one of its 2 slots. `neighbours`: after the swap, device d holds the boxes of first-dimension layer d of a domain 512 layers long and two boxes wide in the second dimension; the lower first-dimension neighbour of a slot lies on device d - 1, the upper on device d + 1, the box beside in the second dimension on device d itself; -1 marks the two ends of the first dimension. `cell_state`: density, pressure and internal energy of every cell are positive.
All inputs are finite; a program needn't handle non-finite values.
Results may differ from the reference program's by a relative error of at most 0.0003.
Values sent between devices are 32-bit elements; how exact they have to be, the bound alone decides.
No kernel may reach another device: no remote copies, remote signals or barrier semaphores. Data moves between devices by JAX's collectives and lax.ppermute only.
A program may use at most 64 MiB of HBM per device.

```python
import math
import jax
import jax.numpy as jnp
from jax import lax

BXC = 32
BYC = 32
BZC = 32
SLOTS = 2
FIELDS = 5
GHOST = 4
RIEMANN_ITERS = 3
NBOX = 1024


def layout(key):
    owners_count = NBOX // SLOTS
    sent = jax.random.randint(jax.random.fold_in(key, 11), (owners_count,), 0, SLOTS).astype(jnp.int32)
    flipped = jax.random.randint(jax.random.fold_in(key, 13), (owners_count,), 0, 2).astype(jnp.int32)
    slot_ids = jnp.arange(NBOX, dtype=jnp.int32)
    device = slot_ids // SLOTS
    within = slot_ids % SLOTS
    across = jnp.bitwise_xor(within, flipped[device])

    def where_is(layer):
        return SLOTS * layer + jnp.bitwise_xor(across, flipped[layer])
    lower = jnp.where(device > 0, where_is(jnp.maximum(device - 1, 0)), -1)
    upper = jnp.where(device < owners_count - 1, where_is(jnp.minimum(device + 1, owners_count - 1)), -1)
    beside = SLOTS * device + (1 - within)
    return (sent, jnp.stack([lower, upper, beside], axis=1).astype(jnp.int32))


def draw_swap_slots(key, part):
    return layout(jax.random.fold_in(key, 5))[0]


def draw_neighbours(key, part):
    return layout(jax.random.fold_in(key, 5))[1]


def draw_cell_state(key, part):
    shape = (NBOX, BXC, BYC, BZC)
    keys = jax.random.split(jax.random.fold_in(key, 3), 5)
    owners_count = NBOX // SLOTS
    place = (jnp.arange(NBOX, dtype=jnp.int32) // SLOTS).astype(jnp.float32) / (owners_count - 1)
    ramp = 1.0 + 2.0 * place
    density = jnp.exp(jax.random.uniform(keys[0], shape, jnp.float32, math.log(0.5), math.log(2.0)))
    velocity = 0.3 * jax.random.truncated_normal(keys[1], -2.0, 2.0, (NBOX, 3, BXC, BYC, BZC), jnp.float32)
    pressure = jnp.exp(jax.random.uniform(keys[2], shape, jnp.float32, math.log(0.5), math.log(2.0)))
    velocity = velocity * ramp[:, None, None, None, None]
    pressure = pressure * (ramp * ramp)[:, None, None, None]
    cold_energy = jax.random.uniform(keys[3], shape, jnp.float32, 0.005, 0.045)
    cold = jax.random.bernoulli(keys[4], 0.1, shape)
    pressure = jnp.where(cold, 0.1 * density * density + 0.4 * density * cold_energy, pressure)
    momentum = density[:, None] * velocity
    energy = (pressure - 0.1 * density * density) / 0.4 + 0.5 * density * jnp.sum(velocity * velocity, axis=1)
    stacked = jnp.concatenate([density[:, None], momentum, energy[:, None]], axis=1)
    return stacked.reshape((NBOX, FIELDS, BXC, BYC * BZC)).astype(jnp.float32)


def setup_inputs(seed: int = 0) -> dict:
    streams_of = jax.random.split(jax.random.key(seed), 4)
    return {
        "cell_state": draw_cell_state(jax.random.fold_in(streams_of[3], 71), 0),
        "swap_slots": draw_swap_slots(jax.random.fold_in(streams_of[3], 71), 0),
        "neighbours": draw_neighbours(jax.random.fold_in(streams_of[3], 71), 0),
    }


EOS_LINEAR = 0.4
EOS_QUAD = 0.1
COURANT = 0.4

def cut(values, start, stop, sweep_axis):
    return lax.slice_in_dim(values, start, stop, axis=sweep_axis)

def minmod(first, second):
    return 0.5 * (jnp.sign(first) + jnp.sign(second)) * jnp.minimum(jnp.abs(first), jnp.abs(second))

def primitives(conserved):
    density = jnp.maximum(conserved[0], 0.05)
    velocity = conserved[1:4] / density
    internal = jnp.maximum(conserved[4] / density - 0.5 * lax.optimization_barrier(jnp.sum(velocity * velocity, axis=0)), 0.05)
    pressure = EOS_LINEAR * density * internal + EOS_QUAD * density * density
    return jnp.concatenate([density[None], velocity, pressure[None]], axis=0)

def fastest(conserved):
    prims = primitives(conserved)
    density = prims[0]
    sound = jnp.sqrt((EOS_QUAD * density * density + (1.0 + EOS_LINEAR) * prims[4]) / density)
    return jnp.max(jnp.abs(prims[1]) + jnp.abs(prims[2]) + jnp.abs(prims[3]) + 3.0 * sound)

def face_states(prims, sweep_axis):
    length = prims.shape[sweep_axis]
    inner = length - 8
    before = cut(prims, 0, length - 3, sweep_axis)
    centre_a = cut(prims, 1, length - 2, sweep_axis)
    centre_b = cut(prims, 2, length - 1, sweep_axis)
    after_b = cut(prims, 3, length, sweep_axis)
    faces = 7.0 / 12.0 * (centre_a + centre_b) - 1.0 / 12.0 * (before + after_b)
    faces = jnp.clip(faces, jnp.minimum(centre_a, centre_b), jnp.maximum(centre_a, centre_b))
    centre = cut(prims, 3, inner + 5, sweep_axis)
    left_edge = cut(faces, 1, inner + 3, sweep_axis)
    right_edge = cut(faces, 2, inner + 4, sweep_axis)
    pressure = prims[4:5]
    normal = prims[sweep_axis:sweep_axis + 1]
    near_diff = cut(pressure, 3, length - 1, sweep_axis) - cut(pressure, 1, length - 3, sweep_axis)
    far_diff = cut(pressure, 4, length, sweep_axis) - cut(pressure, 0, length - 4, sweep_axis)
    far_sum = cut(pressure, 4, length, sweep_axis) + cut(pressure, 0, length - 4, sweep_axis)
    steepness = jnp.abs(near_diff) / (jnp.abs(far_diff) + 0.1 * far_sum)
    squeeze = jnp.maximum(cut(normal, 1, length - 3, sweep_axis) - cut(normal, 3, length - 1, sweep_axis), 0.0)
    shock = jnp.clip((steepness - 0.75) * 4.0, 0.0, 1.0) * squeeze / (squeeze + 0.2)
    widest = jnp.maximum(jnp.maximum(cut(shock, 0, inner + 2, sweep_axis), cut(shock, 1, inner + 3, sweep_axis)), cut(shock, 2, inner + 4, sweep_axis))
    flatten = 1.0 - widest
    down_part = minmod(centre - left_edge, 2.0 * (right_edge - centre))
    up_part = minmod(right_edge - centre, 2.0 * (centre - left_edge))
    lower_val = centre - flatten * down_part
    upper_val = centre + flatten * up_part
    return (cut(upper_val, 0, inner + 1, sweep_axis), cut(lower_val, 1, inner + 2, sweep_axis))

def wave_side(prims):
    density = prims[0]
    pressure = prims[4]
    internal = jnp.maximum((pressure - EOS_QUAD * density * density) / (EOS_LINEAR * density), 0.05)
    impedance = jnp.sqrt(density * (EOS_QUAD * density * density + (1.0 + EOS_LINEAR) * pressure))
    gamma_eff = 1.0 + EOS_LINEAR + EOS_QUAD * density * density / pressure
    growth = (gamma_eff + 1.0) / (2.0 * gamma_eff)
    return (density, pressure, internal, impedance, growth)

def riemann(left_state, right_state, sweep_axis):
    dens_l, pres_l, int_l, imp_l, grow_l = wave_side(left_state)
    dens_r, pres_r, int_r, imp_r, grow_r = wave_side(right_state)
    vel_l = left_state[sweep_axis]
    vel_r = right_state[sweep_axis]
    floor_p = 0.1 * jnp.minimum(pres_l, pres_r)
    p_star = (imp_r * pres_l + imp_l * pres_r + imp_l * imp_r * (vel_l - vel_r)) / (imp_l + imp_r)
    p_star = jnp.maximum(p_star, floor_p)

    def speeds(guess):
        wave_l = imp_l * jnp.sqrt(1.0 + grow_l * (guess / pres_l - 1.0))
        wave_r = imp_r * jnp.sqrt(1.0 + grow_r * (guess / pres_r - 1.0))
        return (wave_l, wave_r)
    for sweep_turn in range(RIEMANN_ITERS):
        wave_l, wave_r = speeds(p_star)
        star_l = vel_l - (p_star - pres_l) / wave_l
        star_r = vel_r + (p_star - pres_r) / wave_r
        slope_l = 2.0 * wave_l ** 3 / (wave_l * wave_l + imp_l * imp_l)
        slope_r = 2.0 * wave_r ** 3 / (wave_r * wave_r + imp_r * imp_r)
        p_star = jnp.maximum(p_star - slope_l * slope_r * (star_r - star_l) / (slope_l + slope_r), floor_p)
    wave_l, wave_r = speeds(p_star)
    star_l = vel_l - (p_star - pres_l) / wave_l
    star_r = vel_r + (p_star - pres_r) / wave_r
    u_star = (wave_l * star_l + wave_r * star_r) / (wave_l + wave_r)
    vol_l = 1.0 / dens_l - (p_star - pres_l) / (wave_l * wave_l)
    vol_r = 1.0 / dens_r - (p_star - pres_r) / (wave_r * wave_r)
    inner_l = jnp.maximum(int_l + 0.5 * (p_star + pres_l) * (1.0 / dens_l - vol_l), 0.1 * int_l)
    inner_r = jnp.maximum(int_r + 0.5 * (p_star + pres_r) * (1.0 / dens_r - vol_r), 0.1 * int_r)
    upwind = u_star >= 0.0
    dens_star = jnp.where(upwind, 1.0 / vol_l, 1.0 / vol_r)
    inner_star = jnp.where(upwind, inner_l, inner_r)
    mass = dens_star * u_star
    kinetic = u_star * u_star
    momenta = []
    for component in range(1, 4):
        if component == sweep_axis:
            momenta.append(mass * u_star + p_star)
        else:
            carried = jnp.where(upwind, left_state[component], right_state[component])
            kinetic = kinetic + carried * carried
            momenta.append(mass * carried)
    energy = u_star * (dens_star * (inner_star + 0.5 * kinetic) + p_star)
    return jnp.stack([mass] + momenta + [energy], axis=0)

def rate(conserved, low_x, high_x, low_y, high_y, ratio):
    extended_x = jnp.concatenate([low_x, conserved, high_x], axis=1)
    extended_y = jnp.concatenate([low_y, conserved, high_y], axis=2)
    extended_z = jnp.concatenate([conserved[..., -GHOST:], conserved, conserved[..., :GHOST]], axis=3)
    tendency = jnp.zeros_like(conserved)
    for sweep_axis, extended in ((1, extended_x), (2, extended_y), (3, extended_z)):
        left_state, right_state = face_states(primitives(extended), sweep_axis)
        fluxes = riemann(left_state, right_state, sweep_axis)
        inner = conserved.shape[sweep_axis]
        tendency = tendency - ratio * (cut(fluxes, 1, inner + 1, sweep_axis) - cut(fluxes, 0, inner, sweep_axis))
    return tendency

def gather_ghosts(box_data, neighbours):
    lower = neighbours[:, 0]
    upper = neighbours[:, 1]
    beside = neighbours[:, 2]
    from_lower = jnp.take(box_data[:, :, -GHOST:], jnp.maximum(lower, 0), axis=0)
    from_upper = jnp.take(box_data[:, :, :GHOST], jnp.maximum(upper, 0), axis=0)
    edge_low = jnp.broadcast_to(box_data[:, :, :1], from_lower.shape)
    edge_high = jnp.broadcast_to(box_data[:, :, -1:], from_upper.shape)
    low_x = jnp.where((lower < 0)[:, None, None, None, None], edge_low, from_lower)
    high_x = jnp.where((upper < 0)[:, None, None, None, None], edge_high, from_upper)
    low_y = jnp.take(box_data[:, :, :, -GHOST:], beside, axis=0)
    high_y = jnp.take(box_data[:, :, :, :GHOST], beside, axis=0)
    return (low_x, high_x, low_y, high_y)

def apply_rate(box_data, neighbours, ratio):
    low_x, high_x, low_y, high_y = gather_ghosts(box_data, neighbours)

    def unpack_rate(bundle):
        return rate(bundle[0], bundle[1], bundle[2], bundle[3], bundle[4], ratio)
    return lax.map(unpack_rate, (box_data, low_x, high_x, low_y, high_y))

def reference(cell_state, swap_slots, neighbours):
    owners_count = NBOX // SLOTS
    box_shape = (FIELDS, BXC, BYC, BZC)
    shaped = cell_state.reshape((owners_count, SLOTS) + box_shape)
    owners = jnp.arange(owners_count, dtype=jnp.int32)
    outgoing = shaped[owners, swap_slots]
    incoming = outgoing[jnp.bitwise_xor(owners, owners_count // 2)]
    chosen = jnp.arange(SLOTS, dtype=jnp.int32)[None, :] == swap_slots[:, None]
    box_data = jnp.where(chosen[:, :, None, None, None, None], incoming[:, None], shaped).reshape((NBOX,) + box_shape)
    ratio = COURANT / jnp.max(lax.map(fastest, box_data))
    first = box_data + apply_rate(box_data, neighbours, ratio)
    result = 0.5 * (box_data + first + apply_rate(first, neighbours, ratio))
    return result.reshape(cell_state.shape)
```

```python
import functools

import jax
import jax.numpy as jnp
from jax import lax
from jax.experimental import pallas as pl
from jax.experimental.pallas import tpu as pltpu
from jax.sharding import PartitionSpec as P

BZC = 32
GHOST = 4
RIEMANN_ITERS = 3
COURANT = 0.4

XC = 32
TILES = 8
COLS = 16
PAD = 48
F32 = jnp.float32


def rcp(value):
    guess = pl.reciprocal(value, approx=True)
    return guess * (2.0 - value * guess)


def prims_of(cons):
    dens = jnp.maximum(cons[0], 0.05)
    inv = rcp(dens)
    v1, v2, v3 = cons[1] * inv, cons[2] * inv, cons[3] * inv
    internal = jnp.maximum(cons[4] * inv - 0.5 * (v1 * v1 + v2 * v2 + v3 * v3), 0.05)
    pres = dens * (0.4 * internal + 0.1 * dens)
    return dens, v1, v2, v3, pres


def face_parts(qm1, q0, q1, q2):
    diff = q1 - q0
    step = 0.5 * diff - (1.0 / 12.0) * ((q2 + qm1) - (q0 + q1))
    step = jnp.minimum(jnp.maximum(step, jnp.minimum(diff, 0.0)), jnp.maximum(diff, 0.0))
    return step, diff - step


def shock_of(pm2, pm1, p1, p2, vm1, v1):
    steep = jnp.abs(p1 - pm1) * rcp(jnp.abs(p2 - pm2) + 0.1 * (p2 + pm2))
    squeeze = jnp.maximum(vm1 - v1, 0.0)
    level = jnp.minimum(jnp.maximum(4.0 * steep - 3.0, 0.0), 1.0)
    return level * squeeze * rcp(squeeze + 0.2)


def minmod(first, second):
    return jnp.maximum(
        jnp.minimum(first, jnp.maximum(second, 0.0)), jnp.minimum(second, 0.0)
    )


def edge_states(centre, below, above, flatten):
    down = minmod(below, above + above)
    up = minmod(above, below + below)
    return centre - flatten * down, centre + flatten * up


def wave_side(dens, pres):
    cube = (0.05 * dens) * (dens * dens)
    both = dens * pres
    base = cube + 0.2 * both
    slope = 1.2 * dens + cube * rcp(pres)
    return base, slope, base + slope * pres


def riemann(left, right, normal):
    dens_l, pres_l, vel_l = left[0], left[4], left[normal]
    dens_r, pres_r, vel_r = right[0], right[4], right[normal]
    base_l, slope_l, imp_l = wave_side(dens_l, pres_l)
    base_r, slope_r, imp_r = wave_side(dens_r, pres_r)
    floor_p = 0.1 * jnp.minimum(pres_l, pres_r)
    gap = vel_r - vel_l
    inv_l, inv_r = lax.rsqrt(imp_l), lax.rsqrt(imp_r)
    guess = (pres_l * inv_l + pres_r * inv_r - gap) * rcp(inv_l + inv_r)
    guess = jnp.maximum(guess, floor_p)
    for _ in range(RIEMANN_ITERS):
        inv_l = lax.rsqrt(base_l + slope_l * guess)
        inv_r = lax.rsqrt(base_r + slope_r * guess)
        miss = gap + (guess - pres_l) * inv_l + (guess - pres_r) * inv_r
        weight = (inv_l + inv_l * (imp_l * (inv_l * inv_l))) + (
            inv_r + inv_r * (imp_r * (inv_r * inv_r))
        )
        guess = jnp.maximum(guess - (miss + miss) * rcp(weight), floor_p)
    inv_l = lax.rsqrt(base_l + slope_l * guess)
    inv_r = lax.rsqrt(base_r + slope_r * guess)
    star_l = vel_l - (guess - pres_l) * inv_l
    star_r = vel_r + (guess - pres_r) * inv_r
    speed = (star_l * inv_r + star_r * inv_l) * rcp(inv_l + inv_r)
    upwind = speed >= 0.0
    dens = jnp.where(upwind, dens_l, dens_r)
    pres = jnp.where(upwind, pres_l, pres_r)
    inv = jnp.where(upwind, inv_l, inv_r)
    inv_dens = rcp(dens)
    internal = jnp.maximum(2.5 * (pres * inv_dens - 0.1 * dens), 0.05)
    shrink = (guess - pres) * (inv * inv)
    star = rcp(inv_dens - shrink)
    internal = jnp.maximum(internal + 0.5 * (guess + pres) * shrink, 0.1 * internal)
    mass = star * speed
    kinetic = speed * speed
    momenta = []
    for component in range(1, 4):
        if component == normal:
            momenta.append(mass * speed + guess)
        else:
            carried = jnp.where(upwind, left[component], right[component])
            kinetic = kinetic + carried * carried
            momenta.append(mass * carried)
    energy = mass * (internal + 0.5 * kinetic) + speed * guess
    return [mass] + momenta + [energy]


def fastest_kernel(state_ref, out_ref):
    def step(index, best):
        box, tile = index // TILES, index % TILES
        lanes = pl.ds(pl.multiple_of(tile * 128, 128), 128)
        dens, v1, v2, v3, pres = prims_of([state_ref[box, f, :, lanes] for f in range(5)])
        square = (0.1 * dens * dens + 1.4 * pres) * rcp(dens)
        speed = jnp.abs(v1) + jnp.abs(v2) + jnp.abs(v3) + 3.0 * (square * lax.rsqrt(square))
        return jnp.maximum(best, speed)

    best = lax.fori_loop(0, COLS, step, jnp.zeros((XC, 128), F32))
    best = jnp.maximum(jnp.maximum(best[:8], best[8:16]), jnp.maximum(best[16:24], best[24:]))
    out_ref[...] = best


def plane_kernel(rows, state_ref, out_ref, prim, near, far, shock, low, high, flux):
    shape = (rows, 128)
    lane = lax.broadcasted_iota(jnp.int32, shape, 1)
    depth = lane % BZC

    def y_ahead(get, tile, steps):
        nxt = lax.rem(tile + 1, COLS)
        return pltpu.roll(
            jnp.where(lane < 32 * steps, get(nxt), get(tile)), 128 - 32 * steps, 1
        )

    def y_back(get, tile, steps):
        prv = lax.rem(tile + COLS - 1, COLS)
        return pltpu.roll(jnp.where(lane >= 128 - 32 * steps, get(prv), get(tile)), 32 * steps, 1)

    def z_ahead(value, steps):
        return jnp.where(
            depth < BZC - steps,
            pltpu.roll(value, 128 - steps, 1),
            pltpu.roll(value, BZC - steps, 1),
        )

    def z_back(value, steps):
        return jnp.where(
            depth >= steps, pltpu.roll(value, steps, 1), pltpu.roll(value, 128 + steps - BZC, 1)
        )

    def fill(tile, _):
        box, part = tile // TILES, tile % TILES
        lanes = pl.ds(pl.multiple_of(part * 128, 128), 128)
        values = prims_of([state_ref[box, f, :, lanes] for f in range(5)])
        for f in range(5):
            prim[f, tile] = values[f]
        return 0

    lax.fori_loop(0, COLS, fill, 0)

    def y_faces(tile, _):
        for f in range(5):
            get = lambda t, f=f: prim[f, t]
            here = get(tile)
            behind = y_back(get, tile, 1)
            ahead = y_ahead(get, tile, 1)
            second = y_ahead(get, tile, 2)
            near[f, tile], far[f, tile] = face_parts(behind, here, ahead, second)
            if f == 2:
                vel_m, vel_p = behind, ahead
            if f == 4:
                shock[tile] = shock_of(
                    y_back(get, tile, 2), behind, ahead, second, vel_m, vel_p
                )
        return 0

    lax.fori_loop(0, COLS, y_faces, 0)

    def y_states(tile, _):
        get = lambda t: shock[t]
        flatten = 1.0 - jnp.maximum(
            jnp.maximum(y_back(get, tile, 1), shock[tile]), y_ahead(get, tile, 1)
        )
        for f in range(5):
            below = y_back(lambda t, f=f: far[f, t], tile, 1)
            low[f, tile], high[f, tile] = edge_states(prim[f, tile], below, near[f, tile], flatten)
        return 0

    lax.fori_loop(0, COLS, y_states, 0)

    def y_flux(tile, _):
        left = [high[f, tile] for f in range(5)]
        right = [y_ahead(lambda t, f=f: low[f, t], tile, 1) for f in range(5)]
        values = riemann(left, right, 2)
        for f in range(5):
            flux[f, tile] = values[f]
        return 0

    lax.fori_loop(0, COLS, y_flux, 0)

    def z_sweep(tile, _):
        box, part = tile // TILES, tile % TILES
        lanes = pl.ds(pl.multiple_of(part * 128, 128), 128)
        parts = []
        for f in range(5):
            here = prim[f, tile]
            behind, ahead, second = z_back(here, 1), z_ahead(here, 1), z_ahead(here, 2)
            parts.append((here,) + face_parts(behind, here, ahead, second))
            if f == 3:
                vel_m, vel_p = behind, ahead
            if f == 4:
                level = shock_of(z_back(here, 2), behind, ahead, second, vel_m, vel_p)
        flatten = 1.0 - jnp.maximum(jnp.maximum(z_back(level, 1), level), z_ahead(level, 1))
        left, right = [], []
        for here, above, rest in parts:
            lower, upper = edge_states(here, z_back(rest, 1), above, flatten)
            left.append(upper)
            right.append(z_ahead(lower, 1))
        values = riemann(left, right, 3)
        for f in range(5):
            across = values[f] - z_back(values[f], 1)
            along = flux[f, tile] - y_back(lambda t, f=f: flux[f, t], tile, 1)
            out_ref[box, f, :, lanes] = across + along
        return 0

    lax.fori_loop(0, COLS, z_sweep, 0)


def line_kernel(
    stage, slot_ref, ratio_ref, state_ref, below_ref, above_ref, plane_ref, *rest
):
    if stage == 2:
        base_ref, out_ref, prim, near, far, shock, low, high, flux, end_low, end_high, end_flux = rest
    else:
        out_ref, prim, near, far, shock, low, high, flux, end_low, end_high, end_flux = rest

    def faces(tile, _):
        box, part = tile // TILES, tile % TILES
        lanes = pl.ds(pl.multiple_of(part * 128, 128), 128)
        start = tile * PAD
        inner = [state_ref[box, f, :, lanes] for f in range(5)]
        below_slot, above_slot = slot_ref[box, 0], slot_ref[box, 1]
        no_below, no_above = slot_ref[box, 2] != 0, slot_ref[box, 3] != 0
        under, over = [], []
        for f in range(5):
            first = jnp.broadcast_to(state_ref[box, f, 0:1, lanes], (GHOST, 128))
            last = jnp.broadcast_to(state_ref[box, f, XC - 1 : XC, lanes], (GHOST, 128))
            under.append(jnp.where(no_below, first, below_ref[below_slot, f, :, lanes]))
            over.append(jnp.where(no_above, last, above_ref[above_slot, f, :, lanes]))
        inner, under, over = prims_of(inner), prims_of(under), prims_of(over)
        for f in range(5):
            prim[f, pl.ds(start, GHOST)] = under[f]
            prim[f, pl.ds(start + GHOST, XC)] = inner[f]
            prim[f, pl.ds(start + GHOST + XC, GHOST)] = over[f]
        for f in range(5):
            here = prim[f, pl.ds(start + 2, 40)]
            behind = prim[f, pl.ds(start + 1, 40)]
            ahead = prim[f, pl.ds(start + 3, 40)]
            second = prim[f, pl.ds(start + 4, 40)]
            near[f, pl.ds(start + 2, 40)], far[f, pl.ds(start + 2, 40)] = face_parts(
                behind, here, ahead, second
            )
            if f == 1:
                vel_m, vel_p = behind, ahead
            if f == 4:
                shock[pl.ds(start + 2, 40)] = shock_of(
                    prim[f, pl.ds(start, 40)], behind, ahead, second, vel_m, vel_p
                )
        flatten = 1.0 - jnp.maximum(
            jnp.maximum(shock[pl.ds(start + 2, 40)], shock[pl.ds(start + 3, 40)]),
            shock[pl.ds(start + 4, 40)],
        )
        for f in range(5):
            lower, upper = edge_states(
                prim[f, pl.ds(start + 3, 40)],
                far[f, pl.ds(start + 2, 40)],
                near[f, pl.ds(start + 3, 40)],
                flatten,
            )
            low[f, pl.ds(start + 3, 40)] = lower
            high[f, pl.ds(start + 3, 40)] = upper
            end_high[f, pl.ds(tile, 1)] = high[f, pl.ds(start + 35, 1)]
            end_low[f, pl.ds(tile, 1)] = low[f, pl.ds(start + 36, 1)]
        return 0

    lax.fori_loop(0, COLS, faces, 0)

    def solve(tile, _):
        start = tile * PAD
        left = [high[f, pl.ds(start + 3, XC)] for f in range(5)]
        right = [low[f, pl.ds(start + 4, XC)] for f in range(5)]
        values = riemann(left, right, 1)
        for f in range(5):
            flux[f, pl.ds(start + 3, XC)] = values[f]
        return 0

    lax.fori_loop(0, COLS, solve, 0)
    values = riemann([end_high[f] for f in range(5)], [end_low[f] for f in range(5)], 1)
    for f in range(5):
        end_flux[f] = values[f]
    ratio = ratio_ref[0]

    def update(tile, _):
        box, part = tile // TILES, tile % TILES
        lanes = pl.ds(pl.multiple_of(part * 128, 128), 128)
        start = tile * PAD
        for f in range(5):
            flux[f, pl.ds(start + 35, 1)] = end_flux[f, pl.ds(tile, 1)]
            across = flux[f, pl.ds(start + 4, XC)] - flux[f, pl.ds(start + 3, XC)]
            rate = ratio * (across + plane_ref[box, f, :, lanes])
            here = state_ref[box, f, :, lanes]
            if stage == 1:
                out_ref[box, f, :, lanes] = here - rate
            else:
                out_ref[box, f, :, lanes] = 0.5 * (base_ref[box, f, :, lanes] + (here - rate))
        return 0

    lax.fori_loop(0, COLS, update, 0)


VMEM = pl.BlockSpec(memory_space=pltpu.VMEM)
SMEM = pl.BlockSpec(memory_space=pltpu.SMEM)
LIMIT = 48 << 20


def params():
    return pltpu.CompilerParams(vmem_limit_bytes=LIMIT)


def fastest(state):
    return pl.pallas_call(
        fastest_kernel,
        out_shape=jax.ShapeDtypeStruct((8, 128), F32),
        in_specs=[VMEM],
        out_specs=VMEM,
        compiler_params=params(),
        name="fastest",
    )(state)


def plane_sweeps(state):
    rows = state.shape[2]
    five = pltpu.VMEM((5, COLS, rows, 128), F32)
    one = pltpu.VMEM((COLS, rows, 128), F32)
    return pl.pallas_call(
        functools.partial(plane_kernel, rows),
        out_shape=jax.ShapeDtypeStruct(state.shape, F32),
        in_specs=[VMEM],
        out_specs=VMEM,
        scratch_shapes=[five, five, five, one, five, five, five],
        compiler_params=params(),
        cost_estimate=pl.CostEstimate(
            flops=60_000_000, bytes_accessed=2_700_000, transcendentals=0
        ),
        name="plane",
    )(state)


def line_sweep(stage, slots, ratio, state, below, above, plane, base=None):
    five = pltpu.VMEM((5, COLS * PAD, 128), F32)
    one = pltpu.VMEM((COLS * PAD, 128), F32)
    end = pltpu.VMEM((5, COLS, 128), F32)
    args = [slots, ratio, state, below, above, plane]
    if stage == 2:
        args.append(base)
    return pl.pallas_call(
        functools.partial(line_kernel, stage),
        out_shape=jax.ShapeDtypeStruct(state.shape, F32),
        in_specs=[SMEM, SMEM] + [VMEM] * (len(args) - 2),
        out_specs=VMEM,
        scratch_shapes=[five, five, five, one, five, five, five, end, end, end],
        compiler_params=params(),
        cost_estimate=pl.CostEstimate(
            flops=30_000_000, bytes_accessed=4_000_000, transcendentals=0
        ),
        name="line",
    )(*args)


def shifted(value, steps):
    count = lax.axis_size("box")
    first, last = max(0, -steps), min(count, count - steps)
    return lax.ppermute(value, "box", [(s, s + steps) for s in range(first, last)])


def all_max(value):
    count = lax.axis_size("box")
    inner = min(count, 32)
    outer = count // inner
    along = [[inner * k + i for k in range(outer)] for i in range(inner)]
    level = [[inner * k + i for i in range(inner)] for k in range(outer)]
    value = jnp.max(lax.all_gather(value, "box", axis_index_groups=level), axis=0)
    value = jnp.max(lax.all_gather(value, "box", axis_index_groups=along), axis=0)
    return jnp.max(value)


def body(cell_state, swap_slots, neighbours):
    slots = cell_state.shape[0]
    count = lax.axis_size("box")
    chosen_slot = swap_slots[0]
    outgoing = lax.dynamic_index_in_dim(cell_state, chosen_slot, 0, keepdims=False)
    incoming = lax.ppermute(outgoing, "box", [(i, i ^ (count // 2)) for i in range(count)])
    ratio = (COURANT / all_max(fastest(cell_state))).reshape(1)
    chosen = jnp.arange(slots, dtype=jnp.int32) == chosen_slot
    after = jnp.where(chosen[:, None, None, None], incoming[None], cell_state)
    own_start = lax.axis_index("box") * slots
    lower, upper = neighbours[:, 0], neighbours[:, 1]
    table = jnp.stack(
        [
            jnp.clip(lower - own_start + slots, 0, slots - 1),
            jnp.clip(upper - own_start - slots, 0, slots - 1),
            (lower < 0).astype(jnp.int32),
            (upper < 0).astype(jnp.int32),
        ],
        axis=1,
    )
    below = shifted(after[:, :, -GHOST:], 1)
    above = shifted(after[:, :, :GHOST], -1)
    first = line_sweep(1, table, ratio, after, below, above, plane_sweeps(after))
    below = shifted(first[:, :, -GHOST:], 1)
    above = shifted(first[:, :, :GHOST], -1)
    return line_sweep(2, table, ratio, first, below, above, plane_sweeps(first), after)


def solution(mesh):
    in_specs = (P("box", None, None, None), P("box"), P("box", None))
    out_specs = P("box", None, None, None)
    return jax.shard_map(body, mesh=mesh, in_specs=in_specs, out_specs=out_specs, check_vma=False)
```

```python
import functools

import jax
import jax.numpy as jnp
from jax import lax
from jax.experimental import pallas as pl
from jax.experimental.pallas import tpu as pltpu
from jax.sharding import PartitionSpec as P

BZC = 32
GHOST = 4
RIEMANN_ITERS = 3
COURANT = 0.4

XC = 32
TILES = 8
COLS = 16
QUARTER = XC // 4
LEVEL = 32
PAD = 48
F32 = jnp.float32


def rcp(value):
    guess = pl.reciprocal(value, approx=True)
    return guess * (2.0 - value * guess)


def prims_of(cons):
    dens = jnp.maximum(cons[0], 0.05)
    inv = rcp(dens)
    v1, v2, v3 = cons[1] * inv, cons[2] * inv, cons[3] * inv
    internal = jnp.maximum(cons[4] * inv - 0.5 * (v1 * v1 + v2 * v2 + v3 * v3), 0.05)
    pres = dens * (0.4 * internal + 0.1 * dens)
    return dens, v1, v2, v3, pres


def face_parts(qm1, q0, q1, q2):
    diff = q1 - q0
    step = 0.5 * diff - (1.0 / 12.0) * ((q2 + qm1) - (q0 + q1))
    step = jnp.minimum(jnp.maximum(step, jnp.minimum(diff, 0.0)), jnp.maximum(diff, 0.0))
    return step, diff - step


def shock_of(pm2, pm1, p1, p2, vm1, v1):
    steep = jnp.abs(p1 - pm1) * rcp(jnp.abs(p2 - pm2) + 0.1 * (p2 + pm2))
    squeeze = jnp.maximum(vm1 - v1, 0.0)
    level = jnp.minimum(jnp.maximum(4.0 * steep - 3.0, 0.0), 1.0)
    return level * squeeze * rcp(squeeze + 0.2)


def minmod(first, second):
    return jnp.maximum(
        jnp.minimum(first, jnp.maximum(second, 0.0)), jnp.minimum(second, 0.0)
    )


def edge_states(centre, below, above, flatten):
    down = minmod(below, above + above)
    up = minmod(above, below + below)
    return centre - flatten * down, centre + flatten * up


def wave_side(dens, pres):
    cube = (0.05 * dens) * (dens * dens)
    both = dens * pres
    base = cube + 0.2 * both
    slope = 1.2 * dens + cube * rcp(pres)
    return base, slope, base + slope * pres


def riemann(left, right, normal):
    dens_l, pres_l, vel_l = left[0], left[4], left[normal]
    dens_r, pres_r, vel_r = right[0], right[4], right[normal]
    base_l, slope_l, imp_l = wave_side(dens_l, pres_l)
    base_r, slope_r, imp_r = wave_side(dens_r, pres_r)
    floor_p = 0.1 * jnp.minimum(pres_l, pres_r)
    gap = vel_r - vel_l
    inv_l, inv_r = lax.rsqrt(imp_l), lax.rsqrt(imp_r)
    guess = (pres_l * inv_l + pres_r * inv_r - gap) * rcp(inv_l + inv_r)
    guess = jnp.maximum(guess, floor_p)
    for _ in range(RIEMANN_ITERS):
        inv_l = lax.rsqrt(base_l + slope_l * guess)
        inv_r = lax.rsqrt(base_r + slope_r * guess)
        miss = gap + (guess - pres_l) * inv_l + (guess - pres_r) * inv_r
        weight = (inv_l + inv_l * (imp_l * (inv_l * inv_l))) + (
            inv_r + inv_r * (imp_r * (inv_r * inv_r))
        )
        guess = jnp.maximum(guess - (miss + miss) * rcp(weight), floor_p)
    inv_l = lax.rsqrt(base_l + slope_l * guess)
    inv_r = lax.rsqrt(base_r + slope_r * guess)
    star_l = vel_l - (guess - pres_l) * inv_l
    star_r = vel_r + (guess - pres_r) * inv_r
    speed = (star_l * inv_r + star_r * inv_l) * rcp(inv_l + inv_r)
    upwind = speed >= 0.0
    dens = jnp.where(upwind, dens_l, dens_r)
    pres = jnp.where(upwind, pres_l, pres_r)
    inv = jnp.where(upwind, inv_l, inv_r)
    inv_dens = rcp(dens)
    internal = jnp.maximum(2.5 * (pres * inv_dens - 0.1 * dens), 0.05)
    shrink = (guess - pres) * (inv * inv)
    star = rcp(inv_dens - shrink)
    internal = jnp.maximum(internal + 0.5 * (guess + pres) * shrink, 0.1 * internal)
    mass = star * speed
    kinetic = speed * speed
    momenta = []
    for component in range(1, 4):
        if component == normal:
            momenta.append(mass * speed + guess)
        else:
            carried = jnp.where(upwind, left[component], right[component])
            kinetic = kinetic + carried * carried
            momenta.append(mass * carried)
    energy = mass * (internal + 0.5 * kinetic) + speed * guess
    return [mass] + momenta + [energy]


def fastest_kernel(state_ref, out_ref):
    def step(index, best):
        box, tile = index // TILES, index % TILES
        lanes = pl.ds(pl.multiple_of(tile * 128, 128), 128)
        dens, v1, v2, v3, pres = prims_of([state_ref[box, f, :, lanes] for f in range(5)])
        square = (0.1 * dens * dens + 1.4 * pres) * rcp(dens)
        speed = jnp.abs(v1) + jnp.abs(v2) + jnp.abs(v3) + 3.0 * (square * lax.rsqrt(square))
        return jnp.maximum(best, speed)

    best = lax.fori_loop(0, COLS, step, jnp.zeros((XC, 128), F32))
    best = jnp.maximum(jnp.maximum(best[:8], best[8:16]), jnp.maximum(best[16:24], best[24:]))
    out_ref[...] = best


def columns(step, group=1):
    def turn(index, _):
        for k in range(group):
            step(index * group + k)
        return 0

    lax.fori_loop(0, COLS // group, turn, 0)


def plane_kernel(
    rows, state_ref, out_ref, prim, near, far, shock, low, high, flux,
    zprim, znear, zfar, zshock, zlow, zhigh, zflux,
):
    lane = lax.broadcasted_iota(jnp.int32, (rows, 128), 1)
    joined = 128 // rows
    ratio = XC // rows

    def y_ahead(get, tile, steps):
        nxt = lax.rem(tile + 1, COLS)
        return pltpu.roll(
            jnp.where(lane < 32 * steps, get(nxt), get(tile)), 128 - 32 * steps, 1
        )

    def y_back(get, tile, steps):
        prv = lax.rem(tile + COLS - 1, COLS)
        return pltpu.roll(jnp.where(lane >= 128 - 32 * steps, get(prv), get(tile)), 32 * steps, 1)

    def fill(tile):
        box, part = tile // TILES, tile % TILES
        lanes = pl.ds(pl.multiple_of(part * 128, 128), 128)
        values = prims_of([state_ref[box, f, :, lanes] for f in range(5)])
        for f in range(5):
            prim[f, tile] = values[f]

    columns(fill, ratio)

    def turn_in(quad, _):
        for f in range(5):
            turned = prim[f, pl.ds(quad * joined, joined)].reshape(128, 128).T
            for k in range(4):
                start = (quad * 4 + k) * PAD
                zprim[f, pl.ds(start + 8, BZC)] = turned[BZC * k : BZC * (k + 1)]
                zprim[f, pl.ds(start + 6, 2)] = zprim[f, pl.ds(start + 38, 2)]
                zprim[f, pl.ds(start + 40, 2)] = zprim[f, pl.ds(start + 8, 2)]
        return 0

    lax.fori_loop(0, COLS // joined, turn_in, 0)

    def y_faces(tile):
        for f in range(5):
            get = lambda t, f=f: prim[f, t]
            here = get(tile)
            behind = y_back(get, tile, 1)
            ahead = y_ahead(get, tile, 1)
            second = y_ahead(get, tile, 2)
            near[f, tile], far[f, tile] = face_parts(behind, here, ahead, second)
            if f == 2:
                vel_m, vel_p = behind, ahead
            if f == 4:
                shock[tile] = shock_of(
                    y_back(get, tile, 2), behind, ahead, second, vel_m, vel_p
                )

    def z_faces(tile):
        start = tile * PAD
        for f in range(5):
            here = zprim[f, pl.ds(start + 8, BZC)]
            behind = zprim[f, pl.ds(start + 7, BZC)]
            ahead = zprim[f, pl.ds(start + 9, BZC)]
            second = zprim[f, pl.ds(start + 10, BZC)]
            rise, rest = face_parts(behind, here, ahead, second)
            znear[f, pl.ds(start + 8, BZC)] = rise
            zfar[f, pl.ds(start + 8, BZC)] = rest
            zfar[f, pl.ds(start + 7, 1)] = rest[BZC - 1 :]
            if f == 3:
                vel_m, vel_p = behind, ahead
            if f == 4:
                level = shock_of(
                    zprim[f, pl.ds(start + 6, BZC)], behind, ahead, second, vel_m, vel_p
                )
                zshock[pl.ds(start + 8, BZC)] = level
                zshock[pl.ds(start + 7, 1)] = level[BZC - 1 :]
                zshock[pl.ds(start + 40, 1)] = level[:1]

    def both(y_step, z_step):
        def turn(index, _):
            for k in range(ratio):
                y_step(index * ratio + k)
            z_step(index)
            return 0

        lax.fori_loop(0, COLS // ratio, turn, 0)

    both(y_faces, z_faces)

    def y_states(tile):
        get = lambda t: shock[t]
        flatten = 1.0 - jnp.maximum(
            jnp.maximum(y_back(get, tile, 1), shock[tile]), y_ahead(get, tile, 1)
        )
        for f in range(5):
            below = y_back(lambda t, f=f: far[f, t], tile, 1)
            low[f, tile], high[f, tile] = edge_states(prim[f, tile], below, near[f, tile], flatten)

    def z_states(tile):
        start = tile * PAD
        flatten = 1.0 - jnp.maximum(
            jnp.maximum(zshock[pl.ds(start + 7, BZC)], zshock[pl.ds(start + 8, BZC)]),
            zshock[pl.ds(start + 9, BZC)],
        )
        for f in range(5):
            lower, upper = edge_states(
                zprim[f, pl.ds(start + 8, BZC)],
                zfar[f, pl.ds(start + 7, BZC)],
                znear[f, pl.ds(start + 8, BZC)],
                flatten,
            )
            zlow[f, pl.ds(start + 8, BZC)] = lower
            zlow[f, pl.ds(start + 40, 1)] = lower[:1]
            zhigh[f, pl.ds(start + 8, BZC)] = upper

    both(y_states, z_states)

    def y_flux(tile):
        left = [high[f, tile] for f in range(5)]
        right = [y_ahead(lambda t, f=f: low[f, t], tile, 1) for f in range(5)]
        values = riemann(left, right, 2)
        for f in range(5):
            flux[f, tile] = values[f]

    def z_flux(tile):
        start = tile * PAD
        left = [zhigh[f, pl.ds(start + 8, BZC)] for f in range(5)]
        right = [zlow[f, pl.ds(start + 9, BZC)] for f in range(5)]
        values = riemann(left, right, 3)
        for f in range(5):
            zflux[f, pl.ds(start + 8, BZC)] = values[f]
            zflux[f, pl.ds(start + 7, 1)] = values[f][BZC - 1 :]

    both(y_flux, z_flux)

    def turn_out(quad, _):
        for f in range(5):
            across = []
            for k in range(4):
                start = (quad * 4 + k) * PAD
                across.append(zflux[f, pl.ds(start + 8, BZC)] - zflux[f, pl.ds(start + 7, BZC)])
            turned = jnp.concatenate(across, axis=0).T
            for k in range(joined):
                tile = quad * joined + k
                box, part = tile // TILES, tile % TILES
                lanes = pl.ds(pl.multiple_of(part * 128, 128), 128)
                along = flux[f, tile] - y_back(lambda t, f=f: flux[f, t], tile, 1)
                out_ref[box, f, :, lanes] = along + turned[rows * k : rows * (k + 1)]
        return 0

    lax.fori_loop(0, COLS // joined, turn_out, 0)


def whole(refs, box, field, lanes):
    if len(refs) == 1:
        return refs[0][box, field, :, lanes]
    outer, second, third = refs
    return jnp.concatenate(
        [
            outer[box, field, :QUARTER, lanes],
            second[box, field, :, lanes],
            third[box, field, :, lanes],
            outer[box, field, QUARTER:, lanes],
        ],
        axis=0,
    )


def line_kernel(counts, slot_ref, ratio_ref, below_ref, above_ref, *refs):
    groups = []
    for n in counts:
        groups.append(refs[:n])
        refs = refs[n:]
    state, plane, base = groups
    out_ref, prim, near, far, shock, low, high, flux, end_low, end_high, end_flux = refs

    def faces(tile):
        box, part = tile // TILES, tile % TILES
        lanes = pl.ds(pl.multiple_of(part * 128, 128), 128)
        start = tile * PAD
        inner = [whole(state, box, f, lanes) for f in range(5)]
        below_slot, above_slot = slot_ref[box, 0], slot_ref[box, 1]
        no_below, no_above = slot_ref[box, 2] != 0, slot_ref[box, 3] != 0
        under, over = [], []
        for f in range(5):
            first = jnp.broadcast_to(inner[f][:1], (GHOST, 128))
            last = jnp.broadcast_to(inner[f][XC - 1 :], (GHOST, 128))
            under.append(jnp.where(no_below, first, below_ref[below_slot, f, :, lanes]))
            over.append(jnp.where(no_above, last, above_ref[above_slot, f, :, lanes]))
        inner, under, over = prims_of(inner), prims_of(under), prims_of(over)
        for f in range(5):
            prim[f, pl.ds(start, GHOST)] = under[f]
            prim[f, pl.ds(start + GHOST, XC)] = inner[f]
            prim[f, pl.ds(start + GHOST + XC, GHOST)] = over[f]
        for f in range(5):
            here = prim[f, pl.ds(start + 2, 40)]
            behind = prim[f, pl.ds(start + 1, 40)]
            ahead = prim[f, pl.ds(start + 3, 40)]
            second = prim[f, pl.ds(start + 4, 40)]
            near[f, pl.ds(start + 2, 40)], far[f, pl.ds(start + 2, 40)] = face_parts(
                behind, here, ahead, second
            )
            if f == 1:
                vel_m, vel_p = behind, ahead
            if f == 4:
                shock[pl.ds(start + 2, 40)] = shock_of(
                    prim[f, pl.ds(start, 40)], behind, ahead, second, vel_m, vel_p
                )
        flatten = 1.0 - jnp.maximum(
            jnp.maximum(shock[pl.ds(start + 2, 40)], shock[pl.ds(start + 3, 40)]),
            shock[pl.ds(start + 4, 40)],
        )
        for f in range(5):
            lower, upper = edge_states(
                prim[f, pl.ds(start + 3, 40)],
                far[f, pl.ds(start + 2, 40)],
                near[f, pl.ds(start + 3, 40)],
                flatten,
            )
            low[f, pl.ds(start + 3, 40)] = lower
            high[f, pl.ds(start + 3, 40)] = upper
            end_high[f, pl.ds(tile, 1)] = high[f, pl.ds(start + 35, 1)]
            end_low[f, pl.ds(tile, 1)] = low[f, pl.ds(start + 36, 1)]

    columns(faces)

    def solve(tile):
        start = tile * PAD
        left = [high[f, pl.ds(start + 3, XC)] for f in range(5)]
        right = [low[f, pl.ds(start + 4, XC)] for f in range(5)]
        values = riemann(left, right, 1)
        for f in range(5):
            flux[f, pl.ds(start + 3, XC)] = values[f]

    columns(solve, 2)
    values = riemann([end_high[f] for f in range(5)], [end_low[f] for f in range(5)], 1)
    for f in range(5):
        end_flux[f] = values[f]
    ratio = ratio_ref[0]

    def update(tile):
        box, part = tile // TILES, tile % TILES
        lanes = pl.ds(pl.multiple_of(part * 128, 128), 128)
        start = tile * PAD
        for f in range(5):
            flux[f, pl.ds(start + 35, 1)] = end_flux[f, pl.ds(tile, 1)]
            across = flux[f, pl.ds(start + 4, XC)] - flux[f, pl.ds(start + 3, XC)]
            value = whole(state, box, f, lanes) - ratio * (across + whole(plane, box, f, lanes))
            if base:
                value = 0.5 * (whole(base, box, f, lanes) + value)
            out_ref[box, f, :, lanes] = value

    columns(update)


VMEM = pl.BlockSpec(memory_space=pltpu.VMEM)
SMEM = pl.BlockSpec(memory_space=pltpu.SMEM)
LIMIT = 48 << 20


def params():
    return pltpu.CompilerParams(vmem_limit_bytes=LIMIT)


def fastest(state):
    return pl.pallas_call(
        fastest_kernel,
        out_shape=jax.ShapeDtypeStruct((8, 128), F32),
        in_specs=[VMEM],
        out_specs=VMEM,
        compiler_params=params(),
        name="fastest",
    )(state)


def plane_sweeps(state):
    rows = state.shape[2]
    depth = COLS * rows // XC * PAD
    five = pltpu.VMEM((5, COLS, rows, 128), F32)
    one = pltpu.VMEM((COLS, rows, 128), F32)
    five_z = pltpu.VMEM((5, depth, 128), F32)
    one_z = pltpu.VMEM((depth, 128), F32)
    return pl.pallas_call(
        functools.partial(plane_kernel, rows),
        out_shape=jax.ShapeDtypeStruct(state.shape, F32),
        in_specs=[VMEM],
        out_specs=VMEM,
        scratch_shapes=[five, five, five, one, five, five, five]
        + [five_z, five_z, five_z, one_z, five_z, five_z, five_z],
        compiler_params=params(),
        cost_estimate=pl.CostEstimate(
            flops=2_000_000 * rows, bytes_accessed=90_000 * rows, transcendentals=0
        ),
        name="plane",
    )(state)


def line_sweep(slots, ratio, below, above, state, plane, base=()):
    five = pltpu.VMEM((5, COLS * PAD, 128), F32)
    one = pltpu.VMEM((COLS * PAD, 128), F32)
    end = pltpu.VMEM((5, COLS, 128), F32)
    args = [slots, ratio, below, above, *state, *plane, *base]
    shape = (slots.shape[0], 5, XC, TILES * 128)
    return pl.pallas_call(
        functools.partial(line_kernel, (len(state), len(plane), len(base))),
        out_shape=jax.ShapeDtypeStruct(shape, F32),
        in_specs=[SMEM, SMEM] + [VMEM] * (len(args) - 2),
        out_specs=VMEM,
        scratch_shapes=[five, five, five, one, five, five, five, end, end, end],
        compiler_params=params(),
        cost_estimate=pl.CostEstimate(
            flops=30_000_000, bytes_accessed=4_000_000, transcendentals=0
        ),
        name="line",
    )(*args)


def shifted(value, steps):
    count = lax.axis_size("box")
    first, last = max(0, -steps), min(count, count - steps)
    return lax.ppermute(value, "box", [(s, s + steps) for s in range(first, last)])


def level_max(value):
    count = lax.axis_size("box")
    inner = min(count, LEVEL)
    level = [[inner * k + i for i in range(inner)] for k in range(count // inner)]
    return jnp.max(lax.all_gather(value, "box", axis_index_groups=level), axis=0)


def turned(value, levels):
    count = lax.axis_size("box")
    return lax.ppermute(value, "box", [(i, (i + levels * LEVEL) % count) for i in range(count)])


def quarters(value, *wanted):
    parts = [value[..., QUARTER * k : QUARTER * (k + 1), :] for k in wanted]
    return jnp.concatenate(parts, axis=-2) if len(parts) > 1 else parts[0]


def body(cell_state, swap_slots, neighbours):
    slots = cell_state.shape[0]
    count = lax.axis_size("box")
    chosen_slot = swap_slots[0]
    chosen = (jnp.arange(slots, dtype=jnp.int32) == chosen_slot)[:, None, None, None]
    levels = max(1, count // LEVEL)
    outgoing = lax.dynamic_index_in_dim(cell_state, chosen_slot, 0, keepdims=False)

    peak = fastest(cell_state)
    peak = jnp.maximum(peak, turned(peak, 1))
    out_most, out_last, peak = lax.optimization_barrier(
        (quarters(outgoing, 0, 1, 3), quarters(outgoing, 2), peak)
    )
    across = [(i, i ^ (count // 2)) for i in range(count)]
    most = lax.ppermute(out_most, "box", across)
    last = lax.ppermute(out_last, "box", across)
    peak = level_max(peak)
    near = [turned(peak, k) for k in range(2, levels // 2, 2)]
    for value in near:
        peak = jnp.maximum(peak, value)
    final = turned(peak, levels // 2)
    most, peak = lax.optimization_barrier((most, peak))

    own_start = lax.axis_index("box") * slots
    lower, upper = neighbours[:, 0], neighbours[:, 1]
    table = jnp.stack(
        [
            jnp.clip(lower - own_start + slots, 0, slots - 1),
            jnp.clip(upper - own_start - slots, 0, slots - 1),
            (lower < 0).astype(jnp.int32),
            (upper < 0).astype(jnp.int32),
        ],
        axis=1,
    )
    outer = jnp.where(chosen, quarters(most, 0, 2)[None], quarters(cell_state, 0, 3))
    second = jnp.where(chosen, quarters(most, 1)[None], quarters(cell_state, 1))
    below = shifted(outer[:, :, -GHOST:], 1)
    above = shifted(outer[:, :, :GHOST], -1)
    planes = [plane_sweeps(outer), plane_sweeps(second)]
    last, *planes = lax.optimization_barrier((last, *planes))
    third = jnp.where(chosen, last[None], quarters(cell_state, 2))
    planes.append(plane_sweeps(third))
    ratio = (COURANT / jnp.max(jnp.maximum(peak, final))).reshape(1)
    after = (outer, second, third)
    first = line_sweep(table, ratio, below, above, after, planes)
    below = shifted(first[:, :, -GHOST:], 1)
    above = shifted(first[:, :, :GHOST], -1)
    return line_sweep(table, ratio, below, above, (first,), (plane_sweeps(first),), after)


def solution(mesh):
    in_specs = (P("box", None, None, None), P("box"), P("box", None))
    out_specs = P("box", None, None, None)
    return jax.shard_map(body, mesh=mesh, in_specs=in_specs, out_specs=out_specs, check_vma=False)
```

```python
import functools

import jax
import jax.numpy as jnp
from jax import lax
from jax.experimental import pallas as pl
from jax.experimental.pallas import tpu as pltpu
from jax.sharding import PartitionSpec as P

BZC = 32
GHOST = 4
RIEMANN_ITERS = 3
COURANT = 0.4

XC = 32
TILES = 8
COLS = 16
QUARTER = XC // 4
LEVEL = 32
PAD = 48
F32 = jnp.float32


def rcp(value):
    return 1.0 / value


def prims_of(cons):
    dens = jnp.maximum(cons[0], 0.05)
    inv = rcp(dens)
    v1, v2, v3 = cons[1] * inv, cons[2] * inv, cons[3] * inv
    internal = jnp.maximum(cons[4] * inv - 0.5 * (v1 * v1 + v2 * v2 + v3 * v3), 0.05)
    pres = dens * (0.4 * internal + 0.1 * dens)
    return dens, v1, v2, v3, pres


def face_parts(qm1, q0, q1, q2):
    diff = q1 - q0
    step = 0.5 * diff - (1.0 / 12.0) * ((q2 + qm1) - (q0 + q1))
    step = jnp.minimum(jnp.maximum(step, jnp.minimum(diff, 0.0)), jnp.maximum(diff, 0.0))
    return step, diff - step


def shock_of(pm2, pm1, p1, p2, vm1, v1):
    steep = jnp.abs(p1 - pm1) * rcp(jnp.abs(p2 - pm2) + 0.1 * (p2 + pm2))
    squeeze = jnp.maximum(vm1 - v1, 0.0)
    level = jnp.minimum(jnp.maximum(4.0 * steep - 3.0, 0.0), 1.0)
    return level * squeeze * rcp(squeeze + 0.2)


def minmod(first, second):
    return jnp.maximum(
        jnp.minimum(first, jnp.maximum(second, 0.0)), jnp.minimum(second, 0.0)
    )


def edge_states(centre, below, above, flatten):
    down = minmod(below, above + above)
    up = minmod(above, below + below)
    return centre - flatten * down, centre + flatten * up


def wave_side(dens, pres):
    cube = (0.05 * dens) * (dens * dens)
    both = dens * pres
    base = cube + 0.2 * both
    slope = 1.2 * dens + cube * rcp(pres)
    return base, slope, base + slope * pres


def riemann(left, right, normal):
    dens_l, pres_l, vel_l = left[0], left[4], left[normal]
    dens_r, pres_r, vel_r = right[0], right[4], right[normal]
    base_l, slope_l, imp_l = wave_side(dens_l, pres_l)
    base_r, slope_r, imp_r = wave_side(dens_r, pres_r)
    floor_p = 0.1 * jnp.minimum(pres_l, pres_r)
    gap = vel_r - vel_l
    inv_l, inv_r = lax.rsqrt(imp_l), lax.rsqrt(imp_r)
    guess = (pres_l * inv_l + pres_r * inv_r - gap) * rcp(inv_l + inv_r)
    guess = jnp.maximum(guess, floor_p)
    for _ in range(RIEMANN_ITERS):
        inv_l = lax.rsqrt(base_l + slope_l * guess)
        inv_r = lax.rsqrt(base_r + slope_r * guess)
        miss = gap + (guess - pres_l) * inv_l + (guess - pres_r) * inv_r
        weight = (inv_l + inv_l * (imp_l * (inv_l * inv_l))) + (
            inv_r + inv_r * (imp_r * (inv_r * inv_r))
        )
        guess = jnp.maximum(guess - (miss + miss) * rcp(weight), floor_p)
    inv_l = lax.rsqrt(base_l + slope_l * guess)
    inv_r = lax.rsqrt(base_r + slope_r * guess)
    star_l = vel_l - (guess - pres_l) * inv_l
    star_r = vel_r + (guess - pres_r) * inv_r
    speed = (star_l * inv_r + star_r * inv_l) * rcp(inv_l + inv_r)
    upwind = speed >= 0.0
    dens = jnp.where(upwind, dens_l, dens_r)
    pres = jnp.where(upwind, pres_l, pres_r)
    inv = jnp.where(upwind, inv_l, inv_r)
    inv_dens = rcp(dens)
    internal = jnp.maximum(2.5 * (pres * inv_dens - 0.1 * dens), 0.05)
    shrink = (guess - pres) * (inv * inv)
    star = rcp(inv_dens - shrink)
    internal = jnp.maximum(internal + 0.5 * (guess + pres) * shrink, 0.1 * internal)
    mass = star * speed
    kinetic = speed * speed
    momenta = []
    for component in range(1, 4):
        if component == normal:
            momenta.append(mass * speed + guess)
        else:
            carried = jnp.where(upwind, left[component], right[component])
            kinetic = kinetic + carried * carried
            momenta.append(mass * carried)
    energy = mass * (internal + 0.5 * kinetic) + speed * guess
    return [mass] + momenta + [energy]


def fastest_kernel(state_ref, out_ref):
    def step(index, best):
        box, tile = index // TILES, index % TILES
        lanes = pl.ds(pl.multiple_of(tile * 128, 128), 128)
        dens, v1, v2, v3, pres = prims_of([state_ref[box, f, :, lanes] for f in range(5)])
        square = (0.1 * dens * dens + 1.4 * pres) * rcp(dens)
        speed = jnp.abs(v1) + jnp.abs(v2) + jnp.abs(v3) + 3.0 * (square * lax.rsqrt(square))
        return jnp.maximum(best, speed)

    best = lax.fori_loop(0, COLS, step, jnp.zeros((XC, 128), F32))
    best = jnp.maximum(jnp.maximum(best[:8], best[8:16]), jnp.maximum(best[16:24], best[24:]))
    out_ref[...] = best


def columns(step, group=1):
    def turn(index, _):
        for k in range(group):
            step(index * group + k)
        return 0

    lax.fori_loop(0, COLS // group, turn, 0)


def plane_kernel(
    rows, state_ref, out_ref, prim, near, far, shock, low, high, flux,
    zprim, znear, zfar, zshock, zlow, zhigh, zflux,
):
    lane = lax.broadcasted_iota(jnp.int32, (rows, 128), 1)
    joined = 128 // rows
    ratio = XC // rows

    def y_ahead(get, tile, steps):
        nxt = lax.rem(tile + 1, COLS)
        return pltpu.roll(
            jnp.where(lane < 32 * steps, get(nxt), get(tile)), 128 - 32 * steps, 1
        )

    def y_back(get, tile, steps):
        prv = lax.rem(tile + COLS - 1, COLS)
        return pltpu.roll(jnp.where(lane >= 128 - 32 * steps, get(prv), get(tile)), 32 * steps, 1)

    def fill(tile):
        box, part = tile // TILES, tile % TILES
        lanes = pl.ds(pl.multiple_of(part * 128, 128), 128)
        values = prims_of([state_ref[box, f, :, lanes] for f in range(5)])
        for f in range(5):
            prim[f, tile] = values[f]

    columns(fill, ratio)

    def turn_in(quad):
        for f in range(5):
            turned = prim[f, pl.ds(quad * joined, joined)].reshape(128, 128).T
            for k in range(4):
                start = (quad * 4 + k) * PAD
                zprim[f, pl.ds(start + 8, BZC)] = turned[BZC * k : BZC * (k + 1)]
                zprim[f, pl.ds(start + 6, 2)] = zprim[f, pl.ds(start + 38, 2)]
                zprim[f, pl.ds(start + 40, 2)] = zprim[f, pl.ds(start + 8, 2)]

    def y_faces(tile):
        for f in range(5):
            get = lambda t, f=f: prim[f, t]
            here = get(tile)
            behind = y_back(get, tile, 1)
            ahead = y_ahead(get, tile, 1)
            second = y_ahead(get, tile, 2)
            near[f, tile], far[f, tile] = face_parts(behind, here, ahead, second)
            if f == 2:
                vel_m, vel_p = behind, ahead
            if f == 4:
                shock[tile] = shock_of(
                    y_back(get, tile, 2), behind, ahead, second, vel_m, vel_p
                )

    def z_faces(tile):
        start = tile * PAD
        for f in range(5):
            here = zprim[f, pl.ds(start + 8, BZC)]
            behind = zprim[f, pl.ds(start + 7, BZC)]
            ahead = zprim[f, pl.ds(start + 9, BZC)]
            second = zprim[f, pl.ds(start + 10, BZC)]
            rise, rest = face_parts(behind, here, ahead, second)
            znear[f, pl.ds(start + 8, BZC)] = rise
            zfar[f, pl.ds(start + 8, BZC)] = rest
            zfar[f, pl.ds(start + 7, 1)] = rest[BZC - 1 :]
            if f == 3:
                vel_m, vel_p = behind, ahead
            if f == 4:
                level = shock_of(
                    zprim[f, pl.ds(start + 6, BZC)], behind, ahead, second, vel_m, vel_p
                )
                zshock[pl.ds(start + 8, BZC)] = level
                zshock[pl.ds(start + 7, 1)] = level[BZC - 1 :]
                zshock[pl.ds(start + 40, 1)] = level[:1]

    def both(y_step, z_step):
        def turn(index, _):
            for k in range(ratio):
                y_step(index * ratio + k)
            z_step(index)
            return 0

        lax.fori_loop(0, COLS // ratio, turn, 0)

    quads = COLS // joined

    def turn_and_y_faces(quad, _):
        turn_in(quad)
        for k in range(joined):
            y_faces(quad * joined + k)
        return 0

    lax.fori_loop(0, quads, turn_and_y_faces, 0)

    def y_states(tile):
        get = lambda t: shock[t]
        flatten = 1.0 - jnp.maximum(
            jnp.maximum(y_back(get, tile, 1), shock[tile]), y_ahead(get, tile, 1)
        )
        for f in range(5):
            below = y_back(lambda t, f=f: far[f, t], tile, 1)
            low[f, tile], high[f, tile] = edge_states(prim[f, tile], below, near[f, tile], flatten)

    def z_states(tile):
        start = tile * PAD
        flatten = 1.0 - jnp.maximum(
            jnp.maximum(zshock[pl.ds(start + 7, BZC)], zshock[pl.ds(start + 8, BZC)]),
            zshock[pl.ds(start + 9, BZC)],
        )
        for f in range(5):
            lower, upper = edge_states(
                zprim[f, pl.ds(start + 8, BZC)],
                zfar[f, pl.ds(start + 7, BZC)],
                znear[f, pl.ds(start + 8, BZC)],
                flatten,
            )
            zlow[f, pl.ds(start + 8, BZC)] = lower
            zlow[f, pl.ds(start + 40, 1)] = lower[:1]
            zhigh[f, pl.ds(start + 8, BZC)] = upper

    both(y_states, z_faces)

    def y_flux(tile):
        left = [high[f, tile] for f in range(5)]
        right = [y_ahead(lambda t, f=f: low[f, t], tile, 1) for f in range(5)]
        values = riemann(left, right, 2)
        for f in range(5):
            flux[f, tile] = values[f]

    def z_flux(tile):
        start = tile * PAD
        left = [zhigh[f, pl.ds(start + 8, BZC)] for f in range(5)]
        right = [zlow[f, pl.ds(start + 9, BZC)] for f in range(5)]
        values = riemann(left, right, 3)
        for f in range(5):
            zflux[f, pl.ds(start + 8, BZC)] = values[f]
            zflux[f, pl.ds(start + 7, 1)] = values[f][BZC - 1 :]

    both(y_flux, z_states)

    def z_fluxes(quad):
        for k in range(4):
            z_flux(quad * 4 + k)

    def turn_out(quad):
        for f in range(5):
            across = []
            for k in range(4):
                start = (quad * 4 + k) * PAD
                across.append(zflux[f, pl.ds(start + 8, BZC)] - zflux[f, pl.ds(start + 7, BZC)])
            turned = jnp.concatenate(across, axis=0).T
            for k in range(joined):
                tile = quad * joined + k
                box, part = tile // TILES, tile % TILES
                lanes = pl.ds(pl.multiple_of(part * 128, 128), 128)
                along = flux[f, tile] - y_back(lambda t, f=f: flux[f, t], tile, 1)
                out_ref[box, f, :, lanes] = along + turned[rows * k : rows * (k + 1)]

    def solve_and_turn(quad, _):
        turn_out(quad - 1)
        z_fluxes(quad)
        return 0

    z_fluxes(0)
    lax.fori_loop(1, quads, solve_and_turn, 0)
    turn_out(quads - 1)


def whole(refs, box, field, lanes):
    if len(refs) == 1:
        return refs[0][box, field, :, lanes]
    outer, second, third = refs
    return jnp.concatenate(
        [
            outer[box, field, :QUARTER, lanes],
            second[box, field, :, lanes],
            third[box, field, :, lanes],
            outer[box, field, QUARTER:, lanes],
        ],
        axis=0,
    )


def line_kernel(counts, slot_ref, ratio_ref, below_ref, above_ref, *refs):
    groups = []
    for n in counts:
        groups.append(refs[:n])
        refs = refs[n:]
    state, plane, base = groups
    out_ref, prim, near, far, shock, low, high, flux, end_low, end_high, end_flux = refs

    def faces(tile):
        box, part = tile // TILES, tile % TILES
        lanes = pl.ds(pl.multiple_of(part * 128, 128), 128)
        start = tile * PAD
        inner = [whole(state, box, f, lanes) for f in range(5)]
        below_slot, above_slot = slot_ref[box, 0], slot_ref[box, 1]
        no_below, no_above = slot_ref[box, 2] != 0, slot_ref[box, 3] != 0
        under, over = [], []
        for f in range(5):
            first = jnp.broadcast_to(inner[f][:1], (GHOST, 128))
            last = jnp.broadcast_to(inner[f][XC - 1 :], (GHOST, 128))
            under.append(jnp.where(no_below, first, below_ref[below_slot, f, :, lanes]))
            over.append(jnp.where(no_above, last, above_ref[above_slot, f, :, lanes]))
        inner, under, over = prims_of(inner), prims_of(under), prims_of(over)
        for f in range(5):
            prim[f, pl.ds(start, GHOST)] = under[f]
            prim[f, pl.ds(start + GHOST, XC)] = inner[f]
            prim[f, pl.ds(start + GHOST + XC, GHOST)] = over[f]
        for f in range(5):
            here = prim[f, pl.ds(start + 2, 40)]
            behind = prim[f, pl.ds(start + 1, 40)]
            ahead = prim[f, pl.ds(start + 3, 40)]
            second = prim[f, pl.ds(start + 4, 40)]
            near[f, pl.ds(start + 2, 40)], far[f, pl.ds(start + 2, 40)] = face_parts(
                behind, here, ahead, second
            )
            if f == 1:
                vel_m, vel_p = behind, ahead
            if f == 4:
                shock[pl.ds(start + 2, 40)] = shock_of(
                    prim[f, pl.ds(start, 40)], behind, ahead, second, vel_m, vel_p
                )
        flatten = 1.0 - jnp.maximum(
            jnp.maximum(shock[pl.ds(start + 2, 40)], shock[pl.ds(start + 3, 40)]),
            shock[pl.ds(start + 4, 40)],
        )
        for f in range(5):
            lower, upper = edge_states(
                prim[f, pl.ds(start + 3, 40)],
                far[f, pl.ds(start + 2, 40)],
                near[f, pl.ds(start + 3, 40)],
                flatten,
            )
            low[f, pl.ds(start + 3, 40)] = lower
            high[f, pl.ds(start + 3, 40)] = upper
            end_high[f, pl.ds(tile, 1)] = high[f, pl.ds(start + 35, 1)]
            end_low[f, pl.ds(tile, 1)] = low[f, pl.ds(start + 36, 1)]

    columns(faces)

    def solve(tile):
        start = tile * PAD
        left = [high[f, pl.ds(start + 3, XC)] for f in range(5)]
        right = [low[f, pl.ds(start + 4, XC)] for f in range(5)]
        values = riemann(left, right, 1)
        for f in range(5):
            flux[f, pl.ds(start + 3, XC)] = values[f]

    columns(solve, 2)
    values = riemann([end_high[f] for f in range(5)], [end_low[f] for f in range(5)], 1)
    for f in range(5):
        end_flux[f] = values[f]
    ratio = ratio_ref[0]

    def update(tile):
        box, part = tile // TILES, tile % TILES
        lanes = pl.ds(pl.multiple_of(part * 128, 128), 128)
        start = tile * PAD
        for f in range(5):
            flux[f, pl.ds(start + 35, 1)] = end_flux[f, pl.ds(tile, 1)]
            across = flux[f, pl.ds(start + 4, XC)] - flux[f, pl.ds(start + 3, XC)]
            value = whole(state, box, f, lanes) - ratio * (across + whole(plane, box, f, lanes))
            if base:
                value = 0.5 * (whole(base, box, f, lanes) + value)
            out_ref[box, f, :, lanes] = value

    columns(update)


VMEM = pl.BlockSpec(memory_space=pltpu.VMEM)
SMEM = pl.BlockSpec(memory_space=pltpu.SMEM)
LIMIT = 48 << 20


def params():
    return pltpu.CompilerParams(vmem_limit_bytes=LIMIT)


def fastest(state):
    return pl.pallas_call(
        fastest_kernel,
        out_shape=jax.ShapeDtypeStruct((8, 128), F32),
        in_specs=[VMEM],
        out_specs=VMEM,
        compiler_params=params(),
        name="fastest",
    )(state)


def plane_sweeps(state):
    rows = state.shape[2]
    depth = COLS * rows // XC * PAD
    five = pltpu.VMEM((5, COLS, rows, 128), F32)
    one = pltpu.VMEM((COLS, rows, 128), F32)
    five_z = pltpu.VMEM((5, depth, 128), F32)
    one_z = pltpu.VMEM((depth, 128), F32)
    return pl.pallas_call(
        functools.partial(plane_kernel, rows),
        out_shape=jax.ShapeDtypeStruct(state.shape, F32),
        in_specs=[VMEM],
        out_specs=VMEM,
        scratch_shapes=[five, five, five, one, five, five, five]
        + [five_z, five_z, five_z, one_z, five_z, five_z, five_z],
        compiler_params=params(),
        cost_estimate=pl.CostEstimate(
            flops=2_000_000 * rows, bytes_accessed=90_000 * rows, transcendentals=0
        ),
        name="plane",
    )(state)


def line_sweep(slots, ratio, below, above, state, plane, base=()):
    five = pltpu.VMEM((5, COLS * PAD, 128), F32)
    one = pltpu.VMEM((COLS * PAD, 128), F32)
    end = pltpu.VMEM((5, COLS, 128), F32)
    args = [slots, ratio, below, above, *state, *plane, *base]
    shape = (slots.shape[0], 5, XC, TILES * 128)
    return pl.pallas_call(
        functools.partial(line_kernel, (len(state), len(plane), len(base))),
        out_shape=jax.ShapeDtypeStruct(shape, F32),
        in_specs=[SMEM, SMEM] + [VMEM] * (len(args) - 2),
        out_specs=VMEM,
        scratch_shapes=[five, five, five, one, five, five, five, end, end, end],
        compiler_params=params(),
        cost_estimate=pl.CostEstimate(
            flops=30_000_000, bytes_accessed=4_000_000, transcendentals=0
        ),
        name="line",
    )(*args)


def shifted(value, steps):
    count = lax.axis_size("box")
    first, last = max(0, -steps), min(count, count - steps)
    return lax.ppermute(value, "box", [(s, s + steps) for s in range(first, last)])


def level_max(value):
    count = lax.axis_size("box")
    inner = min(count, LEVEL)
    level = [[inner * k + i for i in range(inner)] for k in range(count // inner)]
    return jnp.max(lax.all_gather(value, "box", axis_index_groups=level), axis=0)


def turned(value, levels):
    count = lax.axis_size("box")
    return lax.ppermute(value, "box", [(i, (i + levels * LEVEL) % count) for i in range(count)])


def quarters(value, *wanted):
    parts = [value[..., QUARTER * k : QUARTER * (k + 1), :] for k in wanted]
    return jnp.concatenate(parts, axis=-2) if len(parts) > 1 else parts[0]


def body(cell_state, swap_slots, neighbours):
    slots = cell_state.shape[0]
    count = lax.axis_size("box")
    chosen_slot = swap_slots[0]
    chosen = (jnp.arange(slots, dtype=jnp.int32) == chosen_slot)[:, None, None, None]
    levels = max(1, count // LEVEL)
    outgoing = lax.dynamic_index_in_dim(cell_state, chosen_slot, 0, keepdims=False)

    peak = fastest(cell_state)
    peak = jnp.maximum(peak, turned(peak, 1))
    out_most, out_last, peak = lax.optimization_barrier(
        (quarters(outgoing, 0, 1, 3), quarters(outgoing, 2), peak)
    )
    across = [(i, i ^ (count // 2)) for i in range(count)]
    most = lax.ppermute(out_most, "box", across)
    last = lax.ppermute(out_last, "box", across)
    peak = level_max(peak)
    near = [turned(peak, k) for k in range(2, levels // 2, 2)]
    for value in near:
        peak = jnp.maximum(peak, value)
    final = turned(peak, levels // 2)
    most, peak = lax.optimization_barrier((most, peak))

    own_start = lax.axis_index("box") * slots
    lower, upper = neighbours[:, 0], neighbours[:, 1]
    table = jnp.stack(
        [
            jnp.clip(lower - own_start + slots, 0, slots - 1),
            jnp.clip(upper - own_start - slots, 0, slots - 1),
            (lower < 0).astype(jnp.int32),
            (upper < 0).astype(jnp.int32),
        ],
        axis=1,
    )
    outer = jnp.where(chosen, quarters(most, 0, 2)[None], quarters(cell_state, 0, 3))
    second = jnp.where(chosen, quarters(most, 1)[None], quarters(cell_state, 1))
    below = shifted(outer[:, :, -GHOST:], 1)
    above = shifted(outer[:, :, :GHOST], -1)
    planes = [plane_sweeps(outer), plane_sweeps(second)]
    last, *planes = lax.optimization_barrier((last, *planes))
    third = jnp.where(chosen, last[None], quarters(cell_state, 2))
    planes.append(plane_sweeps(third))
    ratio = (COURANT / jnp.max(jnp.maximum(peak, final))).reshape(1)
    after = (outer, second, third)
    first = line_sweep(table, ratio, below, above, after, planes)
    below = shifted(first[:, :, -GHOST:], 1)
    above = shifted(first[:, :, :GHOST], -1)
    return line_sweep(table, ratio, below, above, (first,), (plane_sweeps(first),), after)


def solution(mesh):
    in_specs = (P("box", None, None, None), P("box"), P("box", None))
    out_specs = P("box", None, None, None)
    return jax.shard_map(body, mesh=mesh, in_specs=in_specs, out_specs=out_specs, check_vma=False)
```

```python
import functools

import jax
import jax.numpy as jnp
from jax import lax
from jax.experimental import pallas as pl
from jax.experimental.pallas import tpu as pltpu
from jax.sharding import PartitionSpec as P

BZC = 32
GHOST = 4
RIEMANN_ITERS = 3
COURANT = 0.4

XC = 32
TILES = 8
COLS = 16
QUARTER = XC // 4
SET_ROWS = 128 // COLS
LEVEL = 32
PAD = 48
F32 = jnp.float32


def rcp(value):
    return 1.0 / value


def prims_of(cons):
    dens = jnp.maximum(cons[0], 0.05)
    inv = rcp(dens)
    v1, v2, v3 = cons[1] * inv, cons[2] * inv, cons[3] * inv
    internal = jnp.maximum(cons[4] * inv - 0.5 * (v1 * v1 + v2 * v2 + v3 * v3), 0.05)
    pres = dens * (0.4 * internal + 0.1 * dens)
    return dens, v1, v2, v3, pres


def face_parts(qm1, q0, q1, q2):
    diff = q1 - q0
    step = 0.5 * diff - (1.0 / 12.0) * ((q2 + qm1) - (q0 + q1))
    step = jnp.minimum(jnp.maximum(step, jnp.minimum(diff, 0.0)), jnp.maximum(diff, 0.0))
    return step, diff - step


def shock_of(pm2, pm1, p1, p2, vm1, v1):
    steep = jnp.abs(p1 - pm1) * rcp(jnp.abs(p2 - pm2) + 0.1 * (p2 + pm2))
    squeeze = jnp.maximum(vm1 - v1, 0.0)
    level = jnp.minimum(jnp.maximum(4.0 * steep - 3.0, 0.0), 1.0)
    return level * squeeze * rcp(squeeze + 0.2)


def minmod(first, second):
    return jnp.maximum(
        jnp.minimum(first, jnp.maximum(second, 0.0)), jnp.minimum(second, 0.0)
    )


def edge_states(centre, below, above, flatten):
    down = minmod(below, above + above)
    up = minmod(above, below + below)
    return centre - flatten * down, centre + flatten * up


def wave_side(dens, pres):
    cube = (0.05 * dens) * (dens * dens)
    both = dens * pres
    base = cube + 0.2 * both
    slope = 1.2 * dens + cube * rcp(pres)
    return base, slope, base + slope * pres


def riemann(left, right, normal):
    dens_l, pres_l, vel_l = left[0], left[4], left[normal]
    dens_r, pres_r, vel_r = right[0], right[4], right[normal]
    base_l, slope_l, imp_l = wave_side(dens_l, pres_l)
    base_r, slope_r, imp_r = wave_side(dens_r, pres_r)
    floor_p = 0.1 * jnp.minimum(pres_l, pres_r)
    gap = vel_r - vel_l
    inv_l, inv_r = lax.rsqrt(imp_l), lax.rsqrt(imp_r)
    guess = (pres_l * inv_l + pres_r * inv_r - gap) * rcp(inv_l + inv_r)
    guess = jnp.maximum(guess, floor_p)
    for _ in range(RIEMANN_ITERS):
        inv_l = lax.rsqrt(base_l + slope_l * guess)
        inv_r = lax.rsqrt(base_r + slope_r * guess)
        miss = gap + (guess - pres_l) * inv_l + (guess - pres_r) * inv_r
        weight = (inv_l + inv_l * (imp_l * (inv_l * inv_l))) + (
            inv_r + inv_r * (imp_r * (inv_r * inv_r))
        )
        guess = jnp.maximum(guess - (miss + miss) * rcp(weight), floor_p)
    inv_l = lax.rsqrt(base_l + slope_l * guess)
    inv_r = lax.rsqrt(base_r + slope_r * guess)
    star_l = vel_l - (guess - pres_l) * inv_l
    star_r = vel_r + (guess - pres_r) * inv_r
    speed = (star_l * inv_r + star_r * inv_l) * rcp(inv_l + inv_r)
    upwind = speed >= 0.0
    dens = jnp.where(upwind, dens_l, dens_r)
    pres = jnp.where(upwind, pres_l, pres_r)
    inv = jnp.where(upwind, inv_l, inv_r)
    inv_dens = rcp(dens)
    internal = jnp.maximum(2.5 * (pres * inv_dens - 0.1 * dens), 0.05)
    shrink = (guess - pres) * (inv * inv)
    star = rcp(inv_dens - shrink)
    internal = jnp.maximum(internal + 0.5 * (guess + pres) * shrink, 0.1 * internal)
    mass = star * speed
    kinetic = speed * speed
    momenta = []
    for component in range(1, 4):
        if component == normal:
            momenta.append(mass * speed + guess)
        else:
            carried = jnp.where(upwind, left[component], right[component])
            kinetic = kinetic + carried * carried
            momenta.append(mass * carried)
    energy = mass * (internal + 0.5 * kinetic) + speed * guess
    return [mass] + momenta + [energy]


def fastest_kernel(state_ref, out_ref):
    def step(index, best):
        box, tile = index // TILES, index % TILES
        lanes = pl.ds(pl.multiple_of(tile * 128, 128), 128)
        dens, v1, v2, v3, pres = prims_of([state_ref[box, f, :, lanes] for f in range(5)])
        square = (0.1 * dens * dens + 1.4 * pres) * rcp(dens)
        speed = jnp.abs(v1) + jnp.abs(v2) + jnp.abs(v3) + 3.0 * (square * lax.rsqrt(square))
        return jnp.maximum(best, speed)

    best = lax.fori_loop(0, COLS, step, jnp.zeros((XC, 128), F32))
    best = jnp.maximum(jnp.maximum(best[:8], best[8:16]), jnp.maximum(best[16:24], best[24:]))
    out_ref[...] = best


def columns(step, group=1):
    def turn(index, _):
        for k in range(group):
            step(index * group + k)
        return 0

    lax.fori_loop(0, COLS // group, turn, 0)


def plane_kernel(
    rows, state_ref, out_ref, prim, ynear, yfar, yshock, ylow, yhigh, yflux,
    znear, zfar, zshock, zlow, zhigh, zflux,
):
    lane_rows = SET_ROWS
    inside = pl.ds(8, BZC)

    def follow(value):
        return pltpu.roll(value, 128 - lane_rows, 1)

    def precede(value):
        return pltpu.roll(value, lane_rows, 1)

    def strip(index):
        steps(pl.ds(pl.multiple_of(index * lane_rows, lane_rows), lane_rows))

    def tile_of(index):
        box, part = divmod(index, TILES)
        return box, pl.ds(part * 128, 128)

    def turn_in(chosen):
        values = []
        for k in range(COLS):
            box, lanes = tile_of(k)
            values.append(prims_of([state_ref[box, f, chosen, lanes] for f in range(5)]))
        for f in range(5):
            swapped = jnp.concatenate([v[f] for v in values], axis=0).T
            for k in range(4):
                here = 2 + k
                prim[f, here, pl.ds(8, BZC)] = swapped[BZC * k : BZC * (k + 1)]
                prim[f, here, pl.ds(6, 2)] = swapped[BZC * (k + 1) - 2 : BZC * (k + 1)]
                prim[f, here, pl.ds(40, 2)] = swapped[BZC * k : BZC * k + 2]

    def z_faces():
        for k in range(4):
            here, start = 2 + k, k * PAD
            column = prim.at[:, here]
            for f in range(5):
                behind, centre = column[f, pl.ds(7, BZC)], column[f, inside]
                ahead, second = column[f, pl.ds(9, BZC)], column[f, pl.ds(10, BZC)]
                rise, rest = face_parts(behind, centre, ahead, second)
                znear[f, pl.ds(start + 8, BZC)] = rise
                zfar[f, pl.ds(start + 8, BZC)] = rest
                zfar[f, pl.ds(start + 7, 1)] = rest[BZC - 1 :]
                if f == 3:
                    vel_m, vel_p = behind, ahead
                if f == 4:
                    level = shock_of(
                        column[f, pl.ds(6, BZC)], behind, ahead, second, vel_m, vel_p
                    )
                    zshock[pl.ds(start + 8, BZC)] = level
                    zshock[pl.ds(start + 7, 1)] = level[BZC - 1 :]
                    zshock[pl.ds(start + 40, 1)] = level[:1]

    def z_states():
        for k in range(4):
            here, start = 2 + k, k * PAD
            flatten = 1.0 - jnp.maximum(
                jnp.maximum(zshock[pl.ds(start + 7, BZC)], zshock[pl.ds(start + 8, BZC)]),
                zshock[pl.ds(start + 9, BZC)],
            )
            for f in range(5):
                lower, upper = edge_states(
                    prim[f, here, inside],
                    zfar[f, pl.ds(start + 7, BZC)],
                    znear[f, pl.ds(start + 8, BZC)],
                    flatten,
                )
                zlow[f, pl.ds(start + 8, BZC)] = lower
                zlow[f, pl.ds(start + 40, 1)] = lower[:1]
                zhigh[f, pl.ds(start + 8, BZC)] = upper

    def z_solves():
        for k in range(4):
            start = k * PAD
            left = [zhigh[f, pl.ds(start + 8, BZC)] for f in range(5)]
            right = [zlow[f, pl.ds(start + 9, BZC)] for f in range(5)]
            values = riemann(left, right, 3)
            for f in range(5):
                zflux[f, pl.ds(start + 8, BZC)] = values[f]
                zflux[f, pl.ds(start + 7, 1)] = values[f][BZC - 1 :]

    def prim_ends():
        for f in range(5):
            for k in range(2):
                prim[f, k, inside] = precede(prim[f, 4 + k, inside])
                prim[f, 6 + k, inside] = follow(prim[f, 2 + k, inside])

    def y_faces():
        for k in range(4):
            here = 2 + k
            for f in range(5):
                behind, centre = prim[f, here - 1, inside], prim[f, here, inside]
                ahead, second = prim[f, here + 1, inside], prim[f, here + 2, inside]
                rise, rest = face_parts(behind, centre, ahead, second)
                ynear[f, k] = rise
                yfar[f, 1 + k] = rest
                if f == 2:
                    vel_m, vel_p = behind, ahead
                if f == 4:
                    yshock[1 + k] = shock_of(
                        prim[f, here - 2, inside], behind, ahead, second, vel_m, vel_p
                    )

    def face_ends():
        for f in range(5):
            yfar[f, 0] = precede(yfar[f, 4])
        yshock[0] = precede(yshock[4])
        yshock[5] = follow(yshock[1])

    def y_states():
        for k in range(4):
            near_by = k
            flatten = 1.0 - jnp.maximum(
                jnp.maximum(yshock[near_by], yshock[near_by + 1]), yshock[near_by + 2]
            )
            for f in range(5):
                lower, upper = edge_states(
                    prim[f, 2 + k, inside],
                    yfar[f, k],
                    ynear[f, k],
                    flatten,
                )
                ylow[f, k] = lower
                yhigh[f, k] = upper

    def state_ends():
        for f in range(5):
            ylow[f, 4] = follow(ylow[f, 0])

    def y_solves():
        for k in range(4):
            left = [yhigh[f, k] for f in range(5)]
            right = [ylow[f, 1 + k] for f in range(5)]
            values = riemann(left, right, 2)
            for f in range(5):
                yflux[f, 1 + k] = values[f]

    def flux_ends():
        for f in range(5):
            yflux[f, 0] = precede(yflux[f, 4])

    def turn_out(chosen):
        for f in range(5):
            total = []
            for k in range(4):
                start = k * PAD
                across = zflux[f, pl.ds(start + 8, BZC)] - zflux[f, pl.ds(start + 7, BZC)]
                total.append(across + (yflux[f, 1 + k] - yflux[f, k]))
            swapped = jnp.concatenate(total, axis=0).T
            for k in range(COLS):
                box, lanes = tile_of(k)
                out_ref[box, f, chosen, lanes] = swapped[lane_rows * k : lane_rows * (k + 1)]

    def steps(chosen):
        turn_in(chosen)
        z_faces()
        prim_ends()
        y_faces()
        face_ends()
        z_states()
        y_states()
        state_ends()
        y_solves()
        flux_ends()
        z_solves()
        turn_out(chosen)

    def turn(index, _):
        strip(index)
        return 0

    lax.fori_loop(0, rows // lane_rows, turn, 0)


def whole(refs, box, field, lanes):
    if len(refs) == 1:
        return refs[0][box, field, :, lanes]
    outer, second, third = refs
    return jnp.concatenate(
        [
            outer[box, field, :QUARTER, lanes],
            second[box, field, :, lanes],
            third[box, field, :, lanes],
            outer[box, field, QUARTER:, lanes],
        ],
        axis=0,
    )


def line_kernel(counts, slot_ref, ratio_ref, below_ref, above_ref, *refs):
    groups = []
    for n in counts:
        groups.append(refs[:n])
        refs = refs[n:]
    state, plane, base = groups
    out_ref, prim, near, far, shock, low, high, flux, end_low, end_high, end_flux = refs

    def faces(tile):
        box, part = tile // TILES, tile % TILES
        lanes = pl.ds(pl.multiple_of(part * 128, 128), 128)
        start = tile * PAD
        inner = [whole(state, box, f, lanes) for f in range(5)]
        below_slot, above_slot = slot_ref[box, 0], slot_ref[box, 1]
        no_below, no_above = slot_ref[box, 2] != 0, slot_ref[box, 3] != 0
        under, over = [], []
        for f in range(5):
            first = jnp.broadcast_to(inner[f][:1], (GHOST, 128))
            last = jnp.broadcast_to(inner[f][XC - 1 :], (GHOST, 128))
            under.append(jnp.where(no_below, first, below_ref[below_slot, f, :, lanes]))
            over.append(jnp.where(no_above, last, above_ref[above_slot, f, :, lanes]))
        inner, under, over = prims_of(inner), prims_of(under), prims_of(over)
        for f in range(5):
            prim[f, pl.ds(start, GHOST)] = under[f]
            prim[f, pl.ds(start + GHOST, XC)] = inner[f]
            prim[f, pl.ds(start + GHOST + XC, GHOST)] = over[f]
        for f in range(5):
            here = prim[f, pl.ds(start + 2, 40)]
            behind = prim[f, pl.ds(start + 1, 40)]
            ahead = prim[f, pl.ds(start + 3, 40)]
            second = prim[f, pl.ds(start + 4, 40)]
            near[f, pl.ds(start + 2, 40)], far[f, pl.ds(start + 2, 40)] = face_parts(
                behind, here, ahead, second
            )
            if f == 1:
                vel_m, vel_p = behind, ahead
            if f == 4:
                shock[pl.ds(start + 2, 40)] = shock_of(
                    prim[f, pl.ds(start, 40)], behind, ahead, second, vel_m, vel_p
                )
        flatten = 1.0 - jnp.maximum(
            jnp.maximum(shock[pl.ds(start + 2, 40)], shock[pl.ds(start + 3, 40)]),
            shock[pl.ds(start + 4, 40)],
        )
        for f in range(5):
            lower, upper = edge_states(
                prim[f, pl.ds(start + 3, 40)],
                far[f, pl.ds(start + 2, 40)],
                near[f, pl.ds(start + 3, 40)],
                flatten,
            )
            low[f, pl.ds(start + 3, 40)] = lower
            high[f, pl.ds(start + 3, 40)] = upper
            end_high[f, pl.ds(tile, 1)] = high[f, pl.ds(start + 35, 1)]
            end_low[f, pl.ds(tile, 1)] = low[f, pl.ds(start + 36, 1)]

    def solve(tile):
        start = tile * PAD
        left = [high[f, pl.ds(start + 3, XC)] for f in range(5)]
        right = [low[f, pl.ds(start + 4, XC)] for f in range(5)]
        values = riemann(left, right, 1)
        for f in range(5):
            flux[f, pl.ds(start + 3, XC)] = values[f]

    def faces_and_solve(tile):
        faces(tile)
        solve(tile)

    columns(faces_and_solve, 4)
    values = riemann([end_high[f] for f in range(5)], [end_low[f] for f in range(5)], 1)
    for f in range(5):
        end_flux[f] = values[f]
    ratio = ratio_ref[0]

    def update(tile):
        box, part = tile // TILES, tile % TILES
        lanes = pl.ds(pl.multiple_of(part * 128, 128), 128)
        start = tile * PAD
        for f in range(5):
            flux[f, pl.ds(start + 35, 1)] = end_flux[f, pl.ds(tile, 1)]
            across = flux[f, pl.ds(start + 4, XC)] - flux[f, pl.ds(start + 3, XC)]
            value = whole(state, box, f, lanes) - ratio * (across + whole(plane, box, f, lanes))
            if base:
                value = 0.5 * (whole(base, box, f, lanes) + value)
            out_ref[box, f, :, lanes] = value

    columns(update, 4)


VMEM = pl.BlockSpec(memory_space=pltpu.VMEM)
SMEM = pl.BlockSpec(memory_space=pltpu.SMEM)
LIMIT = 48 << 20


def params():
    return pltpu.CompilerParams(vmem_limit_bytes=LIMIT)


def fastest(state):
    return pl.pallas_call(
        fastest_kernel,
        out_shape=jax.ShapeDtypeStruct((8, 128), F32),
        in_specs=[VMEM],
        out_specs=VMEM,
        compiler_params=params(),
        name="fastest",
    )(state)


def plane_sweeps(state):
    rows = state.shape[2]

    def fields(*shape):
        return pltpu.VMEM((5,) + shape + (128,), F32)

    columns_y = [fields(n, BZC) for n in (4, 5, 5, 4, 5)]
    rows_z = [fields(4 * PAD) for _ in range(5)]
    scratch = [fields(8, PAD)] + columns_y[:2]
    scratch += [pltpu.VMEM((6, BZC, 128), F32)] + columns_y[2:]
    scratch += rows_z[:2] + [pltpu.VMEM((4 * PAD, 128), F32)] + rows_z[2:]
    return pl.pallas_call(
        functools.partial(plane_kernel, rows),
        out_shape=jax.ShapeDtypeStruct(state.shape, F32),
        in_specs=[VMEM],
        out_specs=VMEM,
        scratch_shapes=scratch,
        compiler_params=params(),
        cost_estimate=pl.CostEstimate(
            flops=2_000_000 * rows, bytes_accessed=90_000 * rows, transcendentals=0
        ),
        name="plane",
    )(state)


def line_sweep(slots, ratio, below, above, state, plane, base=()):
    five = pltpu.VMEM((5, COLS * PAD, 128), F32)
    one = pltpu.VMEM((COLS * PAD, 128), F32)
    end = pltpu.VMEM((5, COLS, 128), F32)
    args = [slots, ratio, below, above, *state, *plane, *base]
    shape = (slots.shape[0], 5, XC, TILES * 128)
    return pl.pallas_call(
        functools.partial(line_kernel, (len(state), len(plane), len(base))),
        out_shape=jax.ShapeDtypeStruct(shape, F32),
        in_specs=[SMEM, SMEM] + [VMEM] * (len(args) - 2),
        out_specs=VMEM,
        scratch_shapes=[five, five, five, one, five, five, five, end, end, end],
        compiler_params=params(),
        cost_estimate=pl.CostEstimate(
            flops=30_000_000, bytes_accessed=4_000_000, transcendentals=0
        ),
        name="line",
    )(*args)


def shifted(value, steps):
    count = lax.axis_size("box")
    first, last = max(0, -steps), min(count, count - steps)
    return lax.ppermute(value, "box", [(s, s + steps) for s in range(first, last)])


def level_max(value):
    count = lax.axis_size("box")
    inner = min(count, LEVEL)
    level = [[inner * k + i for i in range(inner)] for k in range(count // inner)]
    return jnp.max(lax.all_gather(value, "box", axis_index_groups=level), axis=0)


def turned(value, levels):
    count = lax.axis_size("box")
    return lax.ppermute(value, "box", [(i, (i + levels * LEVEL) % count) for i in range(count)])


def quarters(value, *wanted):
    parts = [value[..., QUARTER * k : QUARTER * (k + 1), :] for k in wanted]
    return jnp.concatenate(parts, axis=-2) if len(parts) > 1 else parts[0]


def body(cell_state, swap_slots, neighbours):
    slots = cell_state.shape[0]
    count = lax.axis_size("box")
    chosen_slot = swap_slots[0]
    chosen = (jnp.arange(slots, dtype=jnp.int32) == chosen_slot)[:, None, None, None]
    levels = max(1, count // LEVEL)
    outgoing = lax.dynamic_index_in_dim(cell_state, chosen_slot, 0, keepdims=False)

    peak = fastest(cell_state)
    peak = jnp.maximum(peak, turned(peak, 1))
    out_most, out_last, peak = lax.optimization_barrier(
        (quarters(outgoing, 0, 1, 3), quarters(outgoing, 2), peak)
    )
    across = [(i, i ^ (count // 2)) for i in range(count)]
    most = lax.ppermute(out_most, "box", across)
    last = lax.ppermute(out_last, "box", across)
    peak = level_max(peak)
    near = [turned(peak, k) for k in range(2, levels // 2, 2)]
    for value in near:
        peak = jnp.maximum(peak, value)
    final = turned(peak, levels // 2)
    most, peak = lax.optimization_barrier((most, peak))

    own_start = lax.axis_index("box") * slots
    lower, upper = neighbours[:, 0], neighbours[:, 1]
    table = jnp.stack(
        [
            jnp.clip(lower - own_start + slots, 0, slots - 1),
            jnp.clip(upper - own_start - slots, 0, slots - 1),
            (lower < 0).astype(jnp.int32),
            (upper < 0).astype(jnp.int32),
        ],
        axis=1,
    )
    outer = jnp.where(chosen, quarters(most, 0, 2)[None], quarters(cell_state, 0, 3))
    second = jnp.where(chosen, quarters(most, 1)[None], quarters(cell_state, 1))
    below = shifted(outer[:, :, -GHOST:], 1)
    above = shifted(outer[:, :, :GHOST], -1)
    planes = [plane_sweeps(outer), plane_sweeps(second)]
    last, *planes = lax.optimization_barrier((last, *planes))
    third = jnp.where(chosen, last[None], quarters(cell_state, 2))
    planes.append(plane_sweeps(third))
    ratio = (COURANT / jnp.max(jnp.maximum(peak, final))).reshape(1)
    after = (outer, second, third)
    first = line_sweep(table, ratio, below, above, after, planes)
    below = shifted(first[:, :, -GHOST:], 1)
    above = shifted(first[:, :, :GHOST], -1)
    return line_sweep(table, ratio, below, above, (first,), (plane_sweeps(first),), after)


def solution(mesh):
    in_specs = (P("box", None, None, None), P("box"), P("box", None))
    out_specs = P("box", None, None, None)
    return jax.shard_map(body, mesh=mesh, in_specs=in_specs, out_specs=out_specs, check_vma=False)
```

```python
import functools

import jax
import jax.numpy as jnp
from jax import lax
from jax.experimental import pallas as pl
from jax.experimental.pallas import tpu as pltpu
from jax.sharding import PartitionSpec as P

BZC = 32
GHOST = 4
RIEMANN_ITERS = 3
COURANT = 0.4

XC = 32
TILES = 8
COLS = 16
QUARTER = XC // 4
SET_ROWS = 128 // COLS
LEVEL = 32
PAD = 48
F32 = jnp.float32


def rcp(value):
    return 1.0 / value


def prims_of(cons):
    dens = jnp.maximum(cons[0], 0.05)
    inv = rcp(dens)
    v1, v2, v3 = cons[1] * inv, cons[2] * inv, cons[3] * inv
    internal = jnp.maximum(cons[4] * inv - 0.5 * (v1 * v1 + v2 * v2 + v3 * v3), 0.05)
    pres = dens * (0.4 * internal + 0.1 * dens)
    return dens, v1, v2, v3, pres


def face_parts(qm1, q0, q1, q2):
    diff = q1 - q0
    step = 0.5 * diff - (1.0 / 12.0) * ((q2 + qm1) - (q0 + q1))
    step = jnp.minimum(jnp.maximum(step, jnp.minimum(diff, 0.0)), jnp.maximum(diff, 0.0))
    return step, diff - step


def shock_of(pm2, pm1, p1, p2, vm1, v1):
    steep = jnp.abs(p1 - pm1) * rcp(jnp.abs(p2 - pm2) + 0.1 * (p2 + pm2))
    squeeze = jnp.maximum(vm1 - v1, 0.0)
    level = jnp.minimum(jnp.maximum(4.0 * steep - 3.0, 0.0), 1.0)
    return level * squeeze * rcp(squeeze + 0.2)


def minmod(first, second):
    return jnp.maximum(
        jnp.minimum(first, jnp.maximum(second, 0.0)), jnp.minimum(second, 0.0)
    )


def edge_states(centre, below, above, flatten):
    down = minmod(below, above + above)
    up = minmod(above, below + below)
    return centre - flatten * down, centre + flatten * up


def wave_side(dens, pres):
    cube = (0.05 * dens) * (dens * dens)
    both = dens * pres
    base = cube + 0.2 * both
    slope = 1.2 * dens + cube * rcp(pres)
    return base, slope, base + slope * pres


def riemann(left, right, normal):
    dens_l, pres_l, vel_l = left[0], left[4], left[normal]
    dens_r, pres_r, vel_r = right[0], right[4], right[normal]
    base_l, slope_l, imp_l = wave_side(dens_l, pres_l)
    base_r, slope_r, imp_r = wave_side(dens_r, pres_r)
    floor_p = 0.1 * jnp.minimum(pres_l, pres_r)
    gap = vel_r - vel_l
    inv_l, inv_r = lax.rsqrt(imp_l), lax.rsqrt(imp_r)
    guess = (pres_l * inv_l + pres_r * inv_r - gap) * rcp(inv_l + inv_r)
    guess = jnp.maximum(guess, floor_p)
    for _ in range(RIEMANN_ITERS):
        inv_l = lax.rsqrt(base_l + slope_l * guess)
        inv_r = lax.rsqrt(base_r + slope_r * guess)
        miss = gap + (guess - pres_l) * inv_l + (guess - pres_r) * inv_r
        weight = (inv_l + inv_l * (imp_l * (inv_l * inv_l))) + (
            inv_r + inv_r * (imp_r * (inv_r * inv_r))
        )
        guess = jnp.maximum(guess - (miss + miss) * rcp(weight), floor_p)
    inv_l = lax.rsqrt(base_l + slope_l * guess)
    inv_r = lax.rsqrt(base_r + slope_r * guess)
    star_l = vel_l - (guess - pres_l) * inv_l
    star_r = vel_r + (guess - pres_r) * inv_r
    speed = (star_l * inv_r + star_r * inv_l) * rcp(inv_l + inv_r)
    upwind = speed >= 0.0
    dens = jnp.where(upwind, dens_l, dens_r)
    pres = jnp.where(upwind, pres_l, pres_r)
    inv = jnp.where(upwind, inv_l, inv_r)
    inv_dens = rcp(dens)
    internal = jnp.maximum(2.5 * (pres * inv_dens - 0.1 * dens), 0.05)
    shrink = (guess - pres) * (inv * inv)
    star = rcp(inv_dens - shrink)
    internal = jnp.maximum(internal + 0.5 * (guess + pres) * shrink, 0.1 * internal)
    mass = star * speed
    kinetic = speed * speed
    momenta = []
    for component in range(1, 4):
        if component == normal:
            momenta.append(mass * speed + guess)
        else:
            carried = jnp.where(upwind, left[component], right[component])
            kinetic = kinetic + carried * carried
            momenta.append(mass * carried)
    energy = mass * (internal + 0.5 * kinetic) + speed * guess
    return [mass] + momenta + [energy]


def fastest_kernel(state_ref, out_ref):
    def step(index, best):
        box, tile = index // TILES, index % TILES
        lanes = pl.ds(pl.multiple_of(tile * 128, 128), 128)
        dens, v1, v2, v3, pres = prims_of([state_ref[box, f, :, lanes] for f in range(5)])
        square = (0.1 * dens * dens + 1.4 * pres) * rcp(dens)
        speed = jnp.abs(v1) + jnp.abs(v2) + jnp.abs(v3) + 3.0 * (square * lax.rsqrt(square))
        return jnp.maximum(best, speed)

    best = lax.fori_loop(0, COLS, step, jnp.zeros((XC, 128), F32))
    best = jnp.maximum(jnp.maximum(best[:8], best[8:16]), jnp.maximum(best[16:24], best[24:]))
    out_ref[...] = best


def columns(step, group=1):
    def turn(index, _):
        for k in range(group):
            step(index * group + k)
        return 0

    lax.fori_loop(0, COLS // group, turn, 0)


def plane_kernel(
    rows, state_ref, out_ref, prim, ynear, yfar, yshock, ylow, yhigh, yflux,
    znear, zfar, zshock, zlow, zhigh, zflux,
):
    lane_rows = SET_ROWS
    inside = pl.ds(8, BZC)

    def follow(value):
        return pltpu.roll(value, 128 - lane_rows, 1)

    def precede(value):
        return pltpu.roll(value, lane_rows, 1)

    def strip(index):
        steps(pl.ds(pl.multiple_of(index * lane_rows, lane_rows), lane_rows))

    def tile_of(index):
        box, part = divmod(index, TILES)
        return box, pl.ds(part * 128, 128)

    def turn_in(chosen):
        values = []
        for k in range(COLS):
            box, lanes = tile_of(k)
            values.append(prims_of([state_ref[box, f, chosen, lanes] for f in range(5)]))
        for f in range(5):
            swapped = jnp.concatenate([v[f] for v in values], axis=0).T
            for k in range(4):
                here = 2 + k
                prim[f, here, pl.ds(8, BZC)] = swapped[BZC * k : BZC * (k + 1)]
                prim[f, here, pl.ds(6, 2)] = swapped[BZC * (k + 1) - 2 : BZC * (k + 1)]
                prim[f, here, pl.ds(40, 2)] = swapped[BZC * k : BZC * k + 2]

    def z_faces():
        for k in range(4):
            here, start = 2 + k, k * PAD
            column = prim.at[:, here]
            for f in range(5):
                behind, centre = column[f, pl.ds(7, BZC)], column[f, inside]
                ahead, second = column[f, pl.ds(9, BZC)], column[f, pl.ds(10, BZC)]
                rise, rest = face_parts(behind, centre, ahead, second)
                znear[f, pl.ds(start + 8, BZC)] = rise
                zfar[f, pl.ds(start + 8, BZC)] = rest
                zfar[f, pl.ds(start + 7, 1)] = rest[BZC - 1 :]
                if f == 3:
                    vel_m, vel_p = behind, ahead
                if f == 4:
                    level = shock_of(
                        column[f, pl.ds(6, BZC)], behind, ahead, second, vel_m, vel_p
                    )
                    zshock[pl.ds(start + 8, BZC)] = level
                    zshock[pl.ds(start + 7, 1)] = level[BZC - 1 :]
                    zshock[pl.ds(start + 40, 1)] = level[:1]

    def z_states():
        for k in range(4):
            here, start = 2 + k, k * PAD
            flatten = 1.0 - jnp.maximum(
                jnp.maximum(zshock[pl.ds(start + 7, BZC)], zshock[pl.ds(start + 8, BZC)]),
                zshock[pl.ds(start + 9, BZC)],
            )
            for f in range(5):
                lower, upper = edge_states(
                    prim[f, here, inside],
                    zfar[f, pl.ds(start + 7, BZC)],
                    znear[f, pl.ds(start + 8, BZC)],
                    flatten,
                )
                zlow[f, pl.ds(start + 8, BZC)] = lower
                zlow[f, pl.ds(start + 40, 1)] = lower[:1]
                zhigh[f, pl.ds(start + 8, BZC)] = upper

    def z_solves():
        for k in range(4):
            start = k * PAD
            left = [zhigh[f, pl.ds(start + 8, BZC)] for f in range(5)]
            right = [zlow[f, pl.ds(start + 9, BZC)] for f in range(5)]
            values = riemann(left, right, 3)
            for f in range(5):
                zflux[f, pl.ds(start + 8, BZC)] = values[f]
                zflux[f, pl.ds(start + 7, 1)] = values[f][BZC - 1 :]

    def prim_ends():
        for f in range(5):
            for k in range(2):
                prim[f, k, inside] = precede(prim[f, 4 + k, inside])
                prim[f, 6 + k, inside] = follow(prim[f, 2 + k, inside])

    def y_faces():
        for k in range(4):
            here = 2 + k
            for f in range(5):
                behind, centre = prim[f, here - 1, inside], prim[f, here, inside]
                ahead, second = prim[f, here + 1, inside], prim[f, here + 2, inside]
                rise, rest = face_parts(behind, centre, ahead, second)
                ynear[f, k] = rise
                yfar[f, 1 + k] = rest
                if f == 2:
                    vel_m, vel_p = behind, ahead
                if f == 4:
                    yshock[1 + k] = shock_of(
                        prim[f, here - 2, inside], behind, ahead, second, vel_m, vel_p
                    )

    def face_ends():
        for f in range(5):
            yfar[f, 0] = precede(yfar[f, 4])
        yshock[0] = precede(yshock[4])
        yshock[5] = follow(yshock[1])

    def y_states():
        for k in range(4):
            near_by = k
            flatten = 1.0 - jnp.maximum(
                jnp.maximum(yshock[near_by], yshock[near_by + 1]), yshock[near_by + 2]
            )
            for f in range(5):
                lower, upper = edge_states(
                    prim[f, 2 + k, inside],
                    yfar[f, k],
                    ynear[f, k],
                    flatten,
                )
                ylow[f, k] = lower
                yhigh[f, k] = upper

    def state_ends():
        for f in range(5):
            ylow[f, 4] = follow(ylow[f, 0])

    def y_solves():
        for k in range(4):
            left = [yhigh[f, k] for f in range(5)]
            right = [ylow[f, 1 + k] for f in range(5)]
            values = riemann(left, right, 2)
            for f in range(5):
                yflux[f, 1 + k] = values[f]

    def flux_ends():
        for f in range(5):
            yflux[f, 0] = precede(yflux[f, 4])

    def turn_out(chosen):
        for f in range(5):
            total = []
            for k in range(4):
                start = k * PAD
                across = zflux[f, pl.ds(start + 8, BZC)] - zflux[f, pl.ds(start + 7, BZC)]
                total.append(across + (yflux[f, 1 + k] - yflux[f, k]))
            swapped = jnp.concatenate(total, axis=0).T
            for k in range(COLS):
                box, lanes = tile_of(k)
                out_ref[box, f, chosen, lanes] = swapped[lane_rows * k : lane_rows * (k + 1)]

    def steps(chosen):
        turn_in(chosen)
        z_faces()
        prim_ends()
        y_faces()
        face_ends()
        z_states()
        y_states()
        state_ends()
        y_solves()
        flux_ends()
        z_solves()
        turn_out(chosen)

    def turn(index, _):
        strip(index)
        return 0

    lax.fori_loop(0, rows // lane_rows, turn, 0)


def whole(refs, box, field, lanes):
    if len(refs) == 1:
        return refs[0][box, field, :, lanes]
    outer, second, third = refs
    return jnp.concatenate(
        [
            outer[box, field, :QUARTER, lanes],
            second[box, field, :, lanes],
            third[box, field, :, lanes],
            outer[box, field, QUARTER:, lanes],
        ],
        axis=0,
    )


def line_kernel(counts, slot_ref, peak_ref, final_ref, below_ref, above_ref, *refs):
    groups = []
    for n in counts:
        groups.append(refs[:n])
        refs = refs[n:]
    state, plane, base = groups
    out_ref, prim, near, far, shock, low, high, flux, end_low, end_high, end_flux = refs

    def faces(tile):
        box, part = tile // TILES, tile % TILES
        lanes = pl.ds(pl.multiple_of(part * 128, 128), 128)
        start = tile * PAD
        inner = [whole(state, box, f, lanes) for f in range(5)]
        below_slot, above_slot = slot_ref[box, 0], slot_ref[box, 1]
        no_below, no_above = slot_ref[box, 2] != 0, slot_ref[box, 3] != 0
        under, over = [], []
        for f in range(5):
            first = jnp.broadcast_to(inner[f][:1], (GHOST, 128))
            last = jnp.broadcast_to(inner[f][XC - 1 :], (GHOST, 128))
            under.append(jnp.where(no_below, first, below_ref[below_slot, f, :, lanes]))
            over.append(jnp.where(no_above, last, above_ref[above_slot, f, :, lanes]))
        inner, under, over = prims_of(inner), prims_of(under), prims_of(over)
        for f in range(5):
            prim[f, pl.ds(start, GHOST)] = under[f]
            prim[f, pl.ds(start + GHOST, XC)] = inner[f]
            prim[f, pl.ds(start + GHOST + XC, GHOST)] = over[f]
        for f in range(5):
            here = prim[f, pl.ds(start + 2, 40)]
            behind = prim[f, pl.ds(start + 1, 40)]
            ahead = prim[f, pl.ds(start + 3, 40)]
            second = prim[f, pl.ds(start + 4, 40)]
            near[f, pl.ds(start + 2, 40)], far[f, pl.ds(start + 2, 40)] = face_parts(
                behind, here, ahead, second
            )
            if f == 1:
                vel_m, vel_p = behind, ahead
            if f == 4:
                shock[pl.ds(start + 2, 40)] = shock_of(
                    prim[f, pl.ds(start, 40)], behind, ahead, second, vel_m, vel_p
                )
        flatten = 1.0 - jnp.maximum(
            jnp.maximum(shock[pl.ds(start + 2, 40)], shock[pl.ds(start + 3, 40)]),
            shock[pl.ds(start + 4, 40)],
        )
        for f in range(5):
            lower, upper = edge_states(
                prim[f, pl.ds(start + 3, 40)],
                far[f, pl.ds(start + 2, 40)],
                near[f, pl.ds(start + 3, 40)],
                flatten,
            )
            low[f, pl.ds(start + 3, 40)] = lower
            high[f, pl.ds(start + 3, 40)] = upper
            end_high[f, pl.ds(tile, 1)] = high[f, pl.ds(start + 35, 1)]
            end_low[f, pl.ds(tile, 1)] = low[f, pl.ds(start + 36, 1)]

    def solve(tile):
        start = tile * PAD
        left = [high[f, pl.ds(start + 3, XC)] for f in range(5)]
        right = [low[f, pl.ds(start + 4, XC)] for f in range(5)]
        values = riemann(left, right, 1)
        for f in range(5):
            flux[f, pl.ds(start + 3, XC)] = values[f]

    def faces_and_solve(tile):
        faces(tile)
        solve(tile)

    columns(faces_and_solve, 8)
    values = riemann([end_high[f] for f in range(5)], [end_low[f] for f in range(5)], 1)
    for f in range(5):
        end_flux[f] = values[f]
    largest = jnp.max(jnp.maximum(peak_ref[...], final_ref[...]), axis=(0, 1), keepdims=True)
    ratio = jnp.broadcast_to(COURANT / largest, (XC, 128))

    def update(tile):
        box, part = tile // TILES, tile % TILES
        lanes = pl.ds(pl.multiple_of(part * 128, 128), 128)
        start = tile * PAD
        for f in range(5):
            flux[f, pl.ds(start + 35, 1)] = end_flux[f, pl.ds(tile, 1)]
            across = flux[f, pl.ds(start + 4, XC)] - flux[f, pl.ds(start + 3, XC)]
            value = whole(state, box, f, lanes) - ratio * (across + whole(plane, box, f, lanes))
            if base:
                value = 0.5 * (whole(base, box, f, lanes) + value)
            out_ref[box, f, :, lanes] = value

    columns(update, 8)


VMEM = pl.BlockSpec(memory_space=pltpu.VMEM)
SMEM = pl.BlockSpec(memory_space=pltpu.SMEM)
LIMIT = 48 << 20


def params():
    return pltpu.CompilerParams(vmem_limit_bytes=LIMIT)


def fastest(state):
    return pl.pallas_call(
        fastest_kernel,
        out_shape=jax.ShapeDtypeStruct((8, 128), F32),
        in_specs=[VMEM],
        out_specs=VMEM,
        compiler_params=params(),
        name="fastest",
    )(state)


def plane_sweeps(state):
    rows = state.shape[2]

    def fields(*shape):
        return pltpu.VMEM((5,) + shape + (128,), F32)

    columns_y = [fields(n, BZC) for n in (4, 5, 5, 4, 5)]
    rows_z = [fields(4 * PAD) for _ in range(5)]
    scratch = [fields(8, PAD)] + columns_y[:2]
    scratch += [pltpu.VMEM((6, BZC, 128), F32)] + columns_y[2:]
    scratch += rows_z[:2] + [pltpu.VMEM((4 * PAD, 128), F32)] + rows_z[2:]
    return pl.pallas_call(
        functools.partial(plane_kernel, rows),
        out_shape=jax.ShapeDtypeStruct(state.shape, F32),
        in_specs=[VMEM],
        out_specs=VMEM,
        scratch_shapes=scratch,
        compiler_params=params(),
        cost_estimate=pl.CostEstimate(
            flops=2_000_000 * rows, bytes_accessed=90_000 * rows, transcendentals=0
        ),
        name="plane",
    )(state)


def line_sweep(slots, peaks, below, above, state, plane, base=()):
    five = pltpu.VMEM((5, COLS * PAD, 128), F32)
    one = pltpu.VMEM((COLS * PAD, 128), F32)
    end = pltpu.VMEM((5, COLS, 128), F32)
    args = [slots, *peaks, below, above, *state, *plane, *base]
    shape = (slots.shape[0], 5, XC, TILES * 128)
    return pl.pallas_call(
        functools.partial(line_kernel, (len(state), len(plane), len(base))),
        out_shape=jax.ShapeDtypeStruct(shape, F32),
        in_specs=[SMEM] + [VMEM] * (len(args) - 1),
        out_specs=VMEM,
        scratch_shapes=[five, five, five, one, five, five, five, end, end, end],
        compiler_params=params(),
        cost_estimate=pl.CostEstimate(
            flops=30_000_000, bytes_accessed=4_000_000, transcendentals=0
        ),
        name="line",
    )(*args)


def shifted(value, steps):
    count = lax.axis_size("box")
    first, last = max(0, -steps), min(count, count - steps)
    return lax.ppermute(value, "box", [(s, s + steps) for s in range(first, last)])


def level_max(value):
    count = lax.axis_size("box")
    inner = min(count, LEVEL)
    level = [[inner * k + i for i in range(inner)] for k in range(count // inner)]
    return jnp.max(lax.all_gather(value, "box", axis_index_groups=level), axis=0)


def turned(value, levels):
    count = lax.axis_size("box")
    return lax.ppermute(value, "box", [(i, (i + levels * LEVEL) % count) for i in range(count)])


def quarters(value, *wanted):
    parts = [value[..., QUARTER * k : QUARTER * (k + 1), :] for k in wanted]
    return jnp.concatenate(parts, axis=-2) if len(parts) > 1 else parts[0]


def body(cell_state, swap_slots, neighbours):
    slots = cell_state.shape[0]
    count = lax.axis_size("box")
    chosen_slot = swap_slots[0]
    chosen = (jnp.arange(slots, dtype=jnp.int32) == chosen_slot)[:, None, None, None]
    levels = max(1, count // LEVEL)
    outgoing = lax.dynamic_index_in_dim(cell_state, chosen_slot, 0, keepdims=False)

    peak = fastest(cell_state)
    peak = jnp.maximum(peak, turned(peak, 1))
    out_most, out_last, peak = lax.optimization_barrier(
        (quarters(outgoing, 0, 1, 3), quarters(outgoing, 2), peak)
    )
    across = [(i, i ^ (count // 2)) for i in range(count)]
    most = lax.ppermute(out_most, "box", across)
    last = lax.ppermute(out_last, "box", across)
    peak = level_max(peak)
    near = [turned(peak, k) for k in range(2, levels // 2, 2)]
    for value in near:
        peak = jnp.maximum(peak, value)
    final = turned(peak, levels // 2)
    most, peak = lax.optimization_barrier((most, peak))

    own_start = lax.axis_index("box") * slots
    lower, upper = neighbours[:, 0], neighbours[:, 1]
    table = jnp.stack(
        [
            jnp.clip(lower - own_start + slots, 0, slots - 1),
            jnp.clip(upper - own_start - slots, 0, slots - 1),
            (lower < 0).astype(jnp.int32),
            (upper < 0).astype(jnp.int32),
        ],
        axis=1,
    )
    outer = jnp.where(chosen, quarters(most, 0, 2)[None], quarters(cell_state, 0, 3))
    second = jnp.where(chosen, quarters(most, 1)[None], quarters(cell_state, 1))
    below = shifted(outer[:, :, -GHOST:], 1)
    above = shifted(outer[:, :, :GHOST], -1)
    planes = [plane_sweeps(outer), plane_sweeps(second)]
    last, *planes = lax.optimization_barrier((last, *planes))
    third = jnp.where(chosen, last[None], quarters(cell_state, 2))
    planes.append(plane_sweeps(third))
    peaks = (peak, final)
    after = (outer, second, third)
    first = line_sweep(table, peaks, below, above, after, planes)
    below = shifted(first[:, :, -GHOST:], 1)
    above = shifted(first[:, :, :GHOST], -1)
    return line_sweep(table, peaks, below, above, (first,), (plane_sweeps(first),), after)


def solution(mesh):
    in_specs = (P("box", None, None, None), P("box"), P("box", None))
    out_specs = P("box", None, None, None)
    return jax.shard_map(body, mesh=mesh, in_specs=in_specs, out_specs=out_specs, check_vma=False)
```
